32 devices in a mesh: grp: 4 (over y, x), slab: 8 (over z, core).
Axes of the slice: x: 2, y: 2, z: 4, core: 2. Of those that a mesh axis runs over, the one named last changes fastest.
Arguments:
- fields: float32 [64, 64, 8, 128], P('grp', 'slab'), may hold values from -6 to 6
- velocity: int32 [3, 64, 8, 128], P(None, 'slab'), may hold values from -2 to 2
- diffusivity: float32 [64, 8, 128], P('slab'), may hold values from 0.005 to 0.04
- sensor_offsets: int32 [49152], P('slab'), may hold values from 0 to 8191
- sensor_counts: int32 [8], P('slab'), may hold values from 1 to 6144, 16384 in all
- observations: float32 [49152], P('slab'), may hold values from -6 to 6
- noise_scale: float32 [49152], P('slab'), may hold values from 2 to 20
- perturbation: float32 [64, 49152], P('grp', 'slab'), may hold values from -6 to 6
Outputs:
- updated: float32 [64, 64, 8, 128], P('grp', 'slab')
The draws below stay inside these ranges and needn't reach their ends.
Inputs may be any that keep to these rules, and one draw needn't show every extreme that they name: `sensor_counts`: the counts sum to 16384 and the largest is exactly 6144. `sensor_offsets`: slots at or past their slab's count are unused.
All inputs are finite; a program needn't handle non-finite values. No bound on the sum of `sensor_counts` on one device may be relied on, other than what follows from the above.
Results may differ from the reference program's by a relative error of at most 0.00011.
Values sent between devices are 32-bit elements; how exact they have to be, the bound alone decides.
A program may use at most 64 MiB of HBM per device.

```python
import math
import jax
import jax.numpy as jnp
import numpy as np
from jax import lax

PX = 128
PY = 8
MEM_DEV = 16
STEPS = 2
SCAP = 6144
CELLS = 8192
NZ = 64
ENS = 64
OBS = 16384
N_SLAB = 8


def set_ends(drawn, own_key, low, high):
    spot = [jax.random.randint(jax.random.fold_in(own_key, axis), (), 0, length) for axis, length in enumerate(drawn.shape)]
    main_axis = drawn.shape.index(max(drawn.shape))
    neighbour = spot[:main_axis] + [(spot[main_axis] + 1) % drawn.shape[main_axis]] + spot[main_axis + 1:]
    return drawn.at[tuple(spot)].set(low).at[tuple(neighbour)].set(high)


def steps_of(key, dims, split, smallest, high):
    factor_of = 1.0
    for position, shards_of in split:
        steps = jax.random.uniform(jax.random.fold_in(jax.random.fold_in(key, 6), position), (shards_of,), jnp.float32, smallest / len(split), high / len(split))
        factor_of = factor_of * jnp.repeat(jnp.exp(steps), dims[position] // shards_of).reshape((-1,) + (1,) * (len(dims) - 1 - position))
    return factor_of


def split_up(count, total, reach, skew):
    loads = [(1 << 20) // math.isqrt(standing ** skew) + 1 for standing in range(2, count + 1)]
    spare, counts = total - reach - (count - 1), [1] * (count - 1)
    while spare > 0:
        candidates = [i for i in range(count - 1) if counts[i] < reach]
        pool, budget = sum([loads[i] for i in candidates]), spare
        for i in candidates:
            addition = min(reach - counts[i], max(1, budget * loads[i] // pool), spare)
            counts[i] = counts[i] + addition
            spare = spare - addition
    return np.array([reach] + counts)


def uneven_parts(stream_key, number_of, total, reach, slope):
    if number_of == 2:
        one = jax.random.randint(stream_key, (), max(1, total - reach), min(reach, total - 1) + 1)
        return jnp.stack([one, total - one])
    lengths = jnp.asarray(split_up(number_of, total, reach, slope), jnp.int32)
    twos = (number_of - 1) // 2
    donor, taker = lengths[1:1 + 2 * twos:2], lengths[2:2 + 2 * twos:2]
    room = jnp.minimum(donor - 1, reach - taker)
    moved = jax.random.randint(jax.random.fold_in(stream_key, 1), (twos,), 0, 1 << 20) % (room + 1)
    lengths = lengths.at[1:1 + 2 * twos:2].set(donor - moved).at[2:2 + 2 * twos:2].set(taker + moved)
    return lengths[jax.random.permutation(jax.random.fold_in(stream_key, 2), number_of)]


def scatter_about(stream_key, extent, spread, bound, split=(), kind=jnp.bfloat16):
    factor_of = steps_of(stream_key, extent, split, -0.22, 0.18) if split else 1.0
    values = jax.random.normal(stream_key, extent, jnp.float32) * spread * factor_of
    return jnp.minimum(jnp.maximum(values, -bound), bound).astype(kind)


def setup_inputs(seed: int = 0) -> dict:
    key_of = jax.random.split(jax.random.key(seed), 9)
    return {
        "fields": scatter_about(key_of[0], (ENS, NZ, PY, PX), 1.0, 6.0, ((0, 4), (1, 8)), jnp.float32),
        "velocity": set_ends(jax.random.randint(key_of[1], (3, NZ, PY, PX), -2, 3), jax.random.fold_in(key_of[1], 1), -2, 2).astype(jnp.int32),
        "diffusivity": jnp.clip(0.005 + 0.035 * jax.random.uniform(key_of[2], (NZ, PY, PX), jnp.float32) ** steps_of(key_of[2], (NZ, PY, PX), ((0, 8),), -0.2, 0.2), 0.005, 0.04),
        "sensor_offsets": set_ends(jax.random.randint(key_of[3], (N_SLAB * SCAP,), 0, CELLS), jax.random.fold_in(key_of[3], 1), 0, CELLS - 1).astype(jnp.int32),
        "sensor_counts": uneven_parts(key_of[4], N_SLAB, OBS, SCAP, 2).astype(jnp.int32),
        "observations": scatter_about(key_of[5], (N_SLAB * SCAP,), 1.0, 6.0, ((0, 8),), jnp.float32),
        "noise_scale": jnp.clip(jnp.exp(math.log(20.0) - 2.3025851 * jax.random.uniform(key_of[6], (N_SLAB * SCAP,), jnp.float32) ** steps_of(key_of[6], (N_SLAB * SCAP,), ((0, 8),), -0.2, 0.2)), 2.0, 20.0),
        "perturbation": scatter_about(key_of[7], (ENS, N_SLAB * SCAP), 1.0, 6.0, ((0, 4), (1, 8)), jnp.float32),
    }


COURANT = 0.12

def upwind(courant, center, lower_side, upper_side):
    return jnp.maximum(courant, 0.0) * (center - lower_side) + jnp.minimum(courant, 0.0) * (upper_side - center)

def advance(extended, courant, diffusivity):
    center = extended[:, 1:-1]
    below = extended[:, :-2]
    above = extended[:, 2:]
    south = jnp.roll(center, 1, axis=2)
    north = jnp.roll(center, -1, axis=2)
    west = jnp.roll(center, 1, axis=3)
    east = jnp.roll(center, -1, axis=3)
    transport = upwind(courant[0], center, below, above) + upwind(courant[1], center, south, north)
    transport = transport + upwind(courant[2], center, west, east)
    laplace = below + above + south + north + west + east - 6.0 * center
    return center - transport + diffusivity * laplace

def solve_weights(gram_matrix, cross_matrix, spread_root):
    order = gram_matrix.shape[0]
    index_row = jnp.arange(order, dtype=jnp.int32)
    system = jnp.eye(order, dtype=jnp.float32) + gram_matrix

    def factor_column(column, lower_factor):
        row_here = lax.dynamic_slice_in_dim(lower_factor, column, 1, 0)[0]
        needed = lax.dynamic_slice_in_dim(system, column, 1, 1)[:, 0]
        needed = needed - jnp.dot(lower_factor, row_here, precision=lax.Precision.HIGHEST, preferred_element_type=jnp.float32)
        pivot = jnp.sqrt(lax.dynamic_slice_in_dim(needed, column, 1, 0)[0])
        values = jnp.where(index_row >= column, needed / pivot, 0.0)
        marker = (index_row == column).astype(jnp.float32)
        return lower_factor + values[:, None] * marker[None, :]
    lower_factor = lax.fori_loop(0, order, factor_column, jnp.zeros((order, order), jnp.float32))

    def forward_row(row, solved):
        factor_row = lax.dynamic_slice_in_dim(lower_factor, row, 1, 0)[0]
        pivot = lax.dynamic_slice_in_dim(factor_row, row, 1, 0)[0]
        given = lax.dynamic_slice_in_dim(cross_matrix, row, 1, 0)[0]
        value = (given - jnp.dot(factor_row, solved, precision=lax.Precision.HIGHEST, preferred_element_type=jnp.float32)) / pivot
        return lax.dynamic_update_slice_in_dim(solved, value[None, :], row, 0)
    middle = lax.fori_loop(0, order, forward_row, jnp.zeros_like(cross_matrix))

    def backward_row(turn, solved):
        row = order - 1 - turn
        factor_col = lax.dynamic_slice_in_dim(lower_factor, row, 1, 1)[:, 0]
        pivot = lax.dynamic_slice_in_dim(factor_col, row, 1, 0)[0]
        given = lax.dynamic_slice_in_dim(middle, row, 1, 0)[0]
        value = (given - jnp.dot(factor_col, solved, precision=lax.Precision.HIGHEST, preferred_element_type=jnp.float32)) / pivot
        return lax.dynamic_update_slice_in_dim(solved, value[None, :], row, 0)
    result = lax.fori_loop(0, order, backward_row, jnp.zeros_like(cross_matrix))
    return result / spread_root

def reference(fields, velocity, diffusivity, sensor_offsets, sensor_counts, observations, noise_scale, perturbation):
    courant = velocity.astype(jnp.float32) * COURANT

    def evolve(block):
        for counter in range(STEPS):
            extended = jnp.pad(block, ((0, 0), (1, 1), (0, 0), (0, 0)))
            block = advance(extended, courant, diffusivity)
        return block
    evolved = lax.map(evolve, fields.reshape(ENS // MEM_DEV, MEM_DEV, NZ, PY, PX))
    flattened = evolved.reshape(ENS, NZ * PY * PX)
    slab_base = (jnp.arange(N_SLAB, dtype=jnp.int32) * CELLS)[:, None]
    cell_index = (slab_base + sensor_offsets.reshape(N_SLAB, SCAP).astype(jnp.int32)).reshape(-1)
    live_mask = (jnp.arange(SCAP, dtype=jnp.int32)[None, :] < sensor_counts[:, None]).reshape(-1).astype(jnp.float32)
    predicted = jnp.take(flattened, cell_index, axis=1)
    scaled = live_mask * predicted / noise_scale
    misfit = live_mask * ((observations - predicted) / noise_scale + perturbation)
    spread_root = math.sqrt(ENS - 1)
    centered = (scaled - lax.optimization_barrier(jnp.sum(scaled, axis=0)) / ENS) / spread_root
    gram_matrix = jnp.dot(centered, centered.T, precision=lax.Precision.HIGHEST, preferred_element_type=jnp.float32)
    cross_matrix = jnp.dot(centered, misfit.T, precision=lax.Precision.HIGHEST, preferred_element_type=jnp.float32)
    weights = solve_weights(gram_matrix, cross_matrix, spread_root)
    increment = jnp.dot(weights.T, flattened, precision=lax.Precision.HIGHEST, preferred_element_type=jnp.float32)
    return (flattened + increment).reshape(ENS, NZ, PY, PX)
```

```python
import functools

import jax
import jax.numpy as jnp
from jax import lax
from jax.experimental import pallas as pl
from jax.experimental.pallas import tpu as pltpu
from jax.sharding import PartitionSpec as P

STEPS = 2
COURANT = 0.12
PIECES = 4
LANES = 128
BLOCK = 8
MESH = pl.DeviceIdType.MESH
NT = (((1,), (1,)), ((), ()))
NN = (((1,), (0,)), ((), ()))


def split_two(values):
    high = values.astype(jnp.bfloat16).astype(jnp.float32)
    return high, values - high


def spread_low(bt, off):
    rows = lax.broadcasted_iota(jnp.int32, bt.shape, 0)
    bt[...] = jnp.where(rows == off % bt.shape[0], 1.0, 0.0).astype(jnp.bfloat16)


def scatter_group(q, high, both, bt, a2, store):
    members = both.shape[0] // 2
    per_group = a2.shape[0] // (2 * members)
    ratio = bt.shape[0] // LANES
    for k in range(per_group):
        a2[k * 2 * members : (k + 1) * 2 * members, :] = jnp.where(
            high[...] == q * per_group + k, both[...], 0.0
        ).astype(jnp.bfloat16)
    res = lax.dot_general(a2[...], bt[...], NT, preferred_element_type=jnp.float32)
    for k in range(per_group):
        start = 2 * k * members
        added = res[start : start + members] + res[start + members : start + 2 * members]
        for i in range(ratio):
            store(k * ratio + i, added[:, i * LANES : (i + 1) * LANES])


def scatter_weights(high, weight, bt, w_ref):
    rows = w_ref.shape[1]
    wanted = lax.broadcasted_iota(jnp.int32, (rows, high.shape[1]), 0)
    first, second = split_two(jnp.where(wanted == high[...], weight, 0.0))
    stacked = jnp.concatenate([first, second], axis=0).astype(jnp.bfloat16)
    res = lax.dot_general(stacked, bt[...], NT, preferred_element_type=jnp.float32)
    total = res[:rows] + res[rows:]
    for i in range(w_ref.shape[0]):
        w_ref[i] = total[:, i * LANES : (i + 1) * LANES]


def upwind(courant, center, lower_side, upper_side):
    return jnp.maximum(courant, 0.0) * (center - lower_side) + jnp.minimum(courant, 0.0) * (
        upper_side - center
    )


def advance(below, center, above, cz, cy, cx, diffusivity):
    y_size, x_size = center.shape[1:]
    south = pltpu.roll(center, 1, 1)
    north = pltpu.roll(center, y_size - 1, 1)
    west = pltpu.roll(center, 1, 2)
    east = pltpu.roll(center, x_size - 1, 2)
    transport = upwind(cz, center, below, above) + upwind(cy, center, south, north)
    transport = transport + upwind(cx, center, west, east)
    laplace = below + above + south + north + west + east - 6.0 * center
    return center - transport + diffusivity * laplace


def solve_in_place(m_ref):
    order, width = m_ref.shape

    def block(b, carry):
        start = pl.multiple_of(b * BLOCK, BLOCK)
        whole = m_ref[...]
        rows = m_ref[pl.ds(start, BLOCK), :]
        row_id = lax.broadcasted_iota(jnp.int32, (BLOCK, width), 0)
        cols = [jnp.broadcast_to(rows[:, i : i + 1], (BLOCK, width)) for i in range(BLOCK)]
        for j in range(BLOCK):
            inverse = 1.0 / cols[j][j : j + 1, :]
            mine = cols[j]
            here = row_id == j

            def eliminate(t):
                pivot_row = t[j : j + 1, :] * inverse
                return jnp.where(here, pivot_row, t - mine * pivot_row)

            rows = eliminate(rows)
            for i in range(j + 1, BLOCK):
                cols[i] = eliminate(cols[i])
        new = whole
        for j in range(BLOCK):
            new = new - whole[:, j : j + 1] * rows[j : j + 1, :]
        m_ref[...] = pltpu.roll(new, width - BLOCK, 1)
        m_ref[pl.ds(start, BLOCK), :] = pltpu.roll(rows, width - BLOCK, 1)
        return carry

    lax.fori_loop(0, order // BLOCK, block, 0)


def step_kernel(
    groups,
    slabs,
    count_ref,
    off_hbm,
    obs_hbm,
    noise_hbm,
    pert_hbm,
    fields_ref,
    vel_ref,
    dif_ref,
    ret,
    off_ref,
    obs_ref,
    noise_ref,
    pert_ref,
    bt,
    a2,
    both,
    v_ref,
    w_ref,
    ext,
    velx,
    difx,
    mid,
    every,
    xs,
    rhs,
    means,
    acc,
    sums,
    parts,
    m_ref,
    local_sem,
    halo_send,
    halo_recv,
    es_sem,
    er_sem,
    ss_sem,
    sr_sem,
    gs_sem,
    gr_sem,
):
    g, s = lax.axis_index("grp"), lax.axis_index("slab")
    members, planes, ys, xsz = fields_ref.shape
    order = members * groups
    last = planes + STEPS

    loads = [
        pltpu.make_async_copy(source, target, local_sem.at[i])
        for i, (source, target) in enumerate(
            (
                (off_hbm, off_ref),
                (noise_hbm, noise_ref),
                (obs_hbm, obs_ref),
                (pert_hbm, pert_ref),
                (fields_ref, ext.at[:, 2:last]),
                (vel_ref, velx.at[:, 1 : planes + 1]),
                (dif_ref, difx.at[1 : planes + 1]),
            )
        )
    ]
    for copy in loads[4:] + loads[:4]:
        copy.start()

    def group_peer(r):
        return (lax.rem(g + r, groups), s)

    def slab_peer(r):
        return (g, lax.rem(s + r, slabs))

    barrier = pltpu.get_barrier_semaphore()
    for r in range(1, slabs):
        pl.semaphore_signal(barrier, inc=1, device_id=slab_peer(r), device_id_type=MESH)
    for r in range(1, groups):
        pl.semaphore_signal(barrier, inc=1, device_id=group_peer(r), device_id_type=MESH)

    def coefficients(p):
        courant = [velx[c, p].astype(jnp.float32)[None] * COURANT for c in range(3)]
        return courant + [difx[p][None]]

    def first_step(p, carry):
        mid[:, p] = advance(ext[:, p], ext[:, p + 1], ext[:, p + 2], *coefficients(p))
        return carry

    def units(p):
        return pl.ds(p * ys, ys)

    square = groups == 4
    beside = g + 1 - 2 * lax.rem(g, 2)
    above = lax.rem(g + 2, groups)

    def block_copy(kind, p, block, peer):
        return pltpu.make_async_remote_copy(
            src_ref=every.at[units(p), block],
            dst_ref=every.at[units(p), block],
            send_sem=es_sem.at[kind, p],
            recv_sem=er_sem.at[kind, p],
            device_id=(peer, s),
            device_id_type=MESH,
        )

    def own_copies(p):
        if square:
            return [block_copy(1, p, g, beside), block_copy(2, p, g, above)]
        return [block_copy(r, p, g, lax.rem(g + r, groups)) for r in range(1, groups)]

    def forward_copy(p):
        turn = lax.rem(p, 2)
        block = beside + (above - beside) * turn
        return block_copy(3, p, block, above + (beside - above) * turn)

    def forward(p):
        if square:
            block_copy(1 + lax.rem(p, 2), p, g, beside).wait_recv()
            forward_copy(p).start()

    def arrived(p):
        if square:
            block_copy(2 - lax.rem(p, 2), p, g, beside).wait_recv()
            block_copy(3, p, g, beside).wait_recv()
        else:
            for copy in own_copies(p):
                copy.wait_recv()

    def second_step(p, carry):
        res = advance(mid[:, p], mid[:, p + 1], mid[:, p + 2], *coefficients(p + 1))
        every[units(p), g] = jnp.swapaxes(res, 0, 1)
        for copy in own_copies(p):
            copy.start()
        return carry

    for copy in loads[4:]:
        copy.wait()
    lax.fori_loop(2, planes, first_step, 0)
    pl.semaphore_wait(barrier, slabs + groups - 2)

    def halo(sign, k, src, dst):
        return pltpu.make_async_remote_copy(
            src_ref=src,
            dst_ref=dst,
            send_sem=halo_send.at[(sign + 1) // 2, k],
            recv_sem=halo_recv.at[(sign + 1) // 2, k],
            device_id=(g, lax.rem(s + sign + slabs, slabs)),
            device_id_type=MESH,
        )

    up = [
        halo(1, 0, fields_ref.at[:, planes - 2 : planes], ext.at[:, 0:2]),
        halo(1, 1, vel_ref.at[:, planes - 1 : planes], velx.at[:, 0:1]),
        halo(1, 2, dif_ref.at[planes - 1 : planes], difx.at[0:1]),
    ]
    down = [
        halo(-1, 0, fields_ref.at[:, 0:2], ext.at[:, last : last + 2]),
        halo(-1, 1, vel_ref.at[:, 0:1], velx.at[:, planes + 1 : planes + 2]),
        halo(-1, 2, dif_ref.at[0:1], difx.at[planes + 1 : planes + 2]),
    ]

    @pl.when(s < slabs - 1)
    def _():
        for copy in up:
            copy.start()

    @pl.when(s > 0)
    def _():
        for copy in down:
            copy.start()

    lax.fori_loop(2, planes - 2, second_step, 0)

    for copy in loads[0:4]:
        copy.wait()
    spread_low(bt, off_ref[...])
    noise = noise_ref[...]
    slot = lax.broadcasted_iota(jnp.int32, noise.shape, 1)
    inverse = jnp.where(slot < count_ref[0], 1.0 / noise, 0.0)
    first, second = split_two((obs_ref[...] / noise + pert_ref[...]) * inverse)
    both[0:members, :] = first
    both[members : 2 * members, :] = second
    off_ref[...] = off_ref[...] // bt.shape[0]

    @pl.when(s == 0)
    def _():
        ext[:, 0:2] = jnp.zeros((members, 2, ys, xsz), jnp.float32)
        velx[:, 0:1] = jnp.zeros((3, 1, ys, xsz), jnp.int32)
        difx[0:1] = jnp.zeros((1, ys, xsz), jnp.float32)

    @pl.when(s == slabs - 1)
    def _():
        ext[:, last : last + 2] = jnp.zeros((members, 2, ys, xsz), jnp.float32)
        velx[:, planes + 1 : planes + 2] = jnp.zeros((3, 1, ys, xsz), jnp.int32)
        difx[planes + 1 : planes + 2] = jnp.zeros((1, ys, xsz), jnp.float32)

    @pl.when(s > 0)
    def _():
        for copy in up:
            copy.wait_recv()

    @pl.when(s < slabs - 1)
    def _():
        for copy in down:
            copy.wait_recv()

    lax.fori_loop(0, 2, first_step, 0)
    lax.fori_loop(planes, planes + 2, first_step, 0)

    @pl.when(s == 0)
    def _():
        mid[:, 0] = jnp.zeros((members, ys, xsz), jnp.float32)

    @pl.when(s == slabs - 1)
    def _():
        mid[:, planes + 1] = jnp.zeros((members, ys, xsz), jnp.float32)

    lax.fori_loop(planes - 2, planes, second_step, 0)
    lax.fori_loop(0, 2, second_step, 0)
    for p in range(2, planes - 2):
        forward(p)

    per = planes * ys // PIECES

    def scatter_turn(i, carry):
        q = lax.rem(i + 1, PIECES)

        def store(u, value):
            v_ref[q * per + u] = value

        scatter_group(q, off_ref, both, bt, a2, store)
        return carry

    lax.fori_loop(0, PIECES - 1, scatter_turn, 0)
    for p in list(range(planes - 2, planes)) + [0, 1]:
        forward(p)
    scatter_turn(PIECES - 1, 0)
    scatter_weights(off_ref, inverse * inverse, bt, w_ref)

    ratio = w_ref.shape[0]
    acc[...] = jnp.zeros(acc.shape, jnp.float32)

    def plane_sums(i, carry):
        p = lax.rem(i + 2, planes)
        arrived(p)
        base = p * ys * xsz
        for u in range(ys):
            unit = p * ys + u
            x = every[unit].reshape(order, xsz)
            mean = jnp.sum(x, axis=0, keepdims=True) / order
            w = w_ref[u % ratio, pl.ds(p * (ys // ratio) + u // ratio, 1), :]
            means[pl.ds(unit, 1), :] = mean
            mine = every[unit, g]
            first, second = split_two(x - mean)
            high, low = split_two(
                jnp.concatenate([(mine - mean) * w, v_ref[unit] - mine * w], axis=0)
            )
            lanes = pl.ds(pl.multiple_of(base + u * xsz, xsz), xsz)
            xs[0:order, lanes] = first.astype(jnp.bfloat16)
            xs[order : 2 * order, lanes] = second.astype(jnp.bfloat16)
            rhs[0 : 2 * members, u * xsz : (u + 1) * xsz] = high.astype(jnp.bfloat16)
            rhs[2 * members :, u * xsz : (u + 1) * xsz] = low.astype(jnp.bfloat16)
        acc[...] += lax.dot_general(
            rhs[...],
            xs[:, pl.ds(pl.multiple_of(base, ys * xsz), ys * xsz)],
            NT,
            preferred_element_type=jnp.float32,
        )
        return carry

    lax.fori_loop(0, planes, plane_sums, 0)

    sent = (acc[0 : 2 * members] + acc[2 * members :]) / (order - 1)
    sent = sent[:, 0:order] + sent[:, order:]
    sums[s] = jnp.concatenate([sent[0:members], sent[members:]], axis=1)
    s_copies = [
        pltpu.make_async_remote_copy(
            src_ref=sums.at[s],
            dst_ref=sums.at[s],
            send_sem=ss_sem.at[r],
            recv_sem=sr_sem.at[r],
            device_id=slab_peer(r),
            device_id_type=MESH,
        )
        for r in range(1, slabs)
    ]
    for copy in s_copies:
        copy.start()
    for copy in s_copies:
        copy.wait_recv()
    added = sums[0]
    for i in range(1, slabs):
        added = added + sums[i]
    parts[g] = added
    g_copies = [
        pltpu.make_async_remote_copy(
            src_ref=parts.at[g],
            dst_ref=parts.at[g],
            send_sem=gs_sem.at[r],
            recv_sem=gr_sem.at[r],
            device_id=group_peer(r),
            device_id_type=MESH,
        )
        for r in range(1, groups)
    ]
    for copy in g_copies:
        copy.start()
    for copy in g_copies:
        copy.wait_recv()

    width = m_ref.shape[1]
    gram = parts[:, :, 0:order].reshape(order, order)
    diagonal = lax.broadcasted_iota(jnp.int32, gram.shape, 0) == lax.broadcasted_iota(
        jnp.int32, gram.shape, 1
    )
    spare = jnp.zeros((width - order - members, order), jnp.float32)
    cross = jnp.concatenate([added[:, order:], spare], axis=0).T
    m_ref[...] = jnp.concatenate([gram + jnp.where(diagonal, 1.0, 0.0), cross], axis=1)
    solve_in_place(m_ref)

    weights = m_ref[...].T[0:members]
    total = jnp.sum(weights, axis=1, keepdims=True)
    high, low = split_two(weights)
    left = jnp.concatenate(
        [jnp.concatenate([half, half], axis=1) for half in (high, low)], axis=0
    ).astype(jnp.bfloat16)

    def plane_update(p, carry):
        lanes = pl.ds(pl.multiple_of(p * ys * xsz, ys * xsz), ys * xsz)
        res = lax.dot_general(left, xs[:, lanes], NN, preferred_element_type=jnp.float32)
        res = res[0:members] + res[members:]
        new = [
            every[p * ys + u, g]
            + (res[:, u * xsz : (u + 1) * xsz] + total * means[pl.ds(p * ys + u, 1), :])
            for u in range(ys)
        ]
        ret[:, p] = jnp.swapaxes(jnp.stack(new, axis=0), 0, 1)
        return carry

    lax.fori_loop(0, planes, plane_update, 0)

    def sent_plane(p, carry):
        for copy in own_copies(p):
            copy.wait_send()
        if square:
            forward_copy(p).wait_send()
        return carry

    lax.fori_loop(0, planes, sent_plane, 0)
    for copy in s_copies + g_copies:
        copy.wait_send()

    @pl.when(s < slabs - 1)
    def _():
        for copy in up:
            copy.wait_send()

    @pl.when(s > 0)
    def _():
        for copy in down:
            copy.wait_send()


def finish_kernel(ret, out_hbm, sem):
    copy = pltpu.make_async_copy(ret, out_hbm, sem)
    copy.start()
    copy.wait()


def local(
    groups,
    slabs,
    fields,
    velocity,
    diffusivity,
    sensor_offsets,
    sensor_counts,
    observations,
    noise_scale,
    perturbation,
):
    members, planes, ys, xsz = fields.shape
    units = planes * ys
    order = members * groups
    slots = sensor_offsets.shape[0]
    low = 2 * LANES
    highs = units * xsz // low
    width = -(-(order + members) // LANES) * LANES
    vmem = pl.BlockSpec(memory_space=pltpu.VMEM)
    f32 = jnp.float32
    scratch = [
        pltpu.VMEM((1, slots), jnp.int32),
        pltpu.VMEM((1, slots), f32),
        pltpu.VMEM((1, slots), f32),
        pltpu.VMEM((members, slots), f32),
        pltpu.VMEM((low, slots), jnp.bfloat16),
        pltpu.VMEM((highs // PIECES * 2 * members, slots), jnp.bfloat16),
        pltpu.VMEM((2 * members, slots), f32),
        pltpu.VMEM((units, members, xsz), f32),
        pltpu.VMEM((low // LANES, highs, LANES), f32),
        pltpu.VMEM((members, planes + 4, ys, xsz), f32),
        pltpu.VMEM((3, planes + 2, ys, xsz), jnp.int32),
        pltpu.VMEM((planes + 2, ys, xsz), f32),
        pltpu.VMEM((members, planes + 2, ys, xsz), f32),
        pltpu.VMEM((units, groups, members, xsz), f32),
        pltpu.VMEM((2 * order, units * xsz), jnp.bfloat16),
        pltpu.VMEM((4 * members, ys * xsz), jnp.bfloat16),
        pltpu.VMEM((units, xsz), f32),
        pltpu.VMEM((4 * members, 2 * order), f32),
        pltpu.VMEM((slabs, members, 2 * order), f32),
        pltpu.VMEM((groups, members, 2 * order), f32),
        pltpu.VMEM((order, width), f32),
        pltpu.SemaphoreType.DMA((7,)),
        pltpu.SemaphoreType.DMA((2, 3)),
        pltpu.SemaphoreType.DMA((2, 3)),
        pltpu.SemaphoreType.DMA((groups, planes)),
        pltpu.SemaphoreType.DMA((groups, planes)),
        pltpu.SemaphoreType.DMA((slabs,)),
        pltpu.SemaphoreType.DMA((slabs,)),
        pltpu.SemaphoreType.DMA((groups,)),
        pltpu.SemaphoreType.DMA((groups,)),
    ]
    anywhere = pl.BlockSpec(memory_space=pl.ANY)
    ret = pl.pallas_call(
        functools.partial(step_kernel, groups, slabs),
        out_shape=jax.ShapeDtypeStruct(fields.shape, f32),
        in_specs=[pl.BlockSpec(memory_space=pltpu.SMEM)] + [anywhere] * 7,
        out_specs=vmem,
        scratch_shapes=scratch,
        compiler_params=pltpu.CompilerParams(
            collective_id=0, has_side_effects=True, vmem_limit_bytes=56 * 1024 * 1024
        ),
        name="ensemble_step",
    )(
        sensor_counts,
        sensor_offsets[None],
        observations[None],
        noise_scale[None],
        perturbation,
        fields,
        velocity,
        diffusivity,
    )
    return pl.pallas_call(
        finish_kernel,
        out_shape=jax.ShapeDtypeStruct(fields.shape, f32),
        in_specs=[vmem],
        out_specs=anywhere,
        scratch_shapes=[pltpu.SemaphoreType.DMA],
        name="finish",
    )(ret)


def solution(mesh):
    return jax.shard_map(
        functools.partial(local, mesh.shape["grp"], mesh.shape["slab"]),
        mesh=mesh,
        in_specs=(
            P("grp", "slab", None, None),
            P(None, "slab", None, None),
            P("slab", None, None),
            P("slab"),
            P("slab"),
            P("slab"),
            P("slab"),
            P("grp", "slab"),
        ),
        out_specs=P("grp", "slab", None, None),
        check_vma=False,
    )
```

```python
import functools

import jax
import jax.numpy as jnp
from jax import lax
from jax.experimental import pallas as pl
from jax.experimental.pallas import tpu as pltpu
from jax.sharding import PartitionSpec as P

STEPS = 2
COURANT = 0.12
PIECES = 2
TILE = 16
LANES = 128
BLOCK = 8
MESH = pl.DeviceIdType.MESH
NT = (((1,), (1,)), ((), ()))
NN = (((1,), (0,)), ((), ()))


def split_two(values):
    high = values.astype(jnp.bfloat16).astype(jnp.float32)
    return high, values - high


def spread_low(bt, low):
    rows = lax.broadcasted_iota(jnp.int32, low.shape, 0).astype(jnp.float32)
    one, zero = jnp.bfloat16(1.0), jnp.bfloat16(0.0)
    for r in range(0, bt.shape[0], TILE):
        wanted = (rows + r).astype(jnp.bfloat16)
        bt[r : r + TILE, :] = jnp.where(low == wanted, one, zero)


def scatter_group(q, high, both, bt, a2, store):
    rows = both.shape[0]
    members = rows // 2
    per_group = a2.shape[0] // rows
    ratio = bt.shape[0] // LANES
    zero = jnp.bfloat16(0.0)
    for k in range(per_group):
        wanted = (q * per_group + k).astype(jnp.float32).astype(jnp.bfloat16)
        for t in range(0, rows, TILE):
            a2[k * rows + t : k * rows + t + TILE, :] = jnp.where(
                high[...] == wanted, both[t : t + TILE, :], zero
            )
    res = lax.dot_general(a2[...], bt[...], NT, preferred_element_type=jnp.float32)
    for k in range(per_group):
        start = k * rows
        added = res[start : start + members] + res[start + members : start + rows]
        for i in range(ratio):
            store(k * ratio + i, added[:, i * LANES : (i + 1) * LANES])


def scatter_weights(high, weight, bt, w_ref):
    rows = w_ref.shape[1]
    wanted = lax.broadcasted_iota(jnp.int32, (rows, high.shape[1]), 0)
    first, second = split_two(jnp.where(wanted == high, weight, 0.0))
    stacked = jnp.concatenate([first, second], axis=0).astype(jnp.bfloat16)
    res = lax.dot_general(stacked, bt[...], NT, preferred_element_type=jnp.float32)
    total = res[:rows] + res[rows:]
    for i in range(w_ref.shape[0]):
        w_ref[i] = total[:, i * LANES : (i + 1) * LANES]


def upwind(courant, center, lower_side, upper_side):
    return jnp.maximum(courant, 0.0) * (center - lower_side) + jnp.minimum(courant, 0.0) * (
        upper_side - center
    )


def advance(below, center, above, cz, cy, cx, diffusivity):
    y_size, x_size = center.shape[1:]
    south = pltpu.roll(center, 1, 1)
    north = pltpu.roll(center, y_size - 1, 1)
    west = pltpu.roll(center, 1, 2)
    east = pltpu.roll(center, x_size - 1, 2)
    transport = upwind(cz, center, below, above) + upwind(cy, center, south, north)
    transport = transport + upwind(cx, center, west, east)
    laplace = below + above + south + north + west + east - 6.0 * center
    return center - transport + diffusivity * laplace


def solve_in_place(m_ref):
    order, width = m_ref.shape

    def block(b, carry):
        start = pl.multiple_of(b * BLOCK, BLOCK)
        whole = m_ref[...]
        rows = m_ref[pl.ds(start, BLOCK), :]
        row_id = lax.broadcasted_iota(jnp.int32, (BLOCK, width), 0)
        cols = [jnp.broadcast_to(rows[:, i : i + 1], (BLOCK, width)) for i in range(BLOCK)]
        for j in range(BLOCK):
            inverse = 1.0 / cols[j][j : j + 1, :]
            mine = cols[j]
            here = row_id == j

            def eliminate(t):
                pivot_row = t[j : j + 1, :] * inverse
                return jnp.where(here, pivot_row, t - mine * pivot_row)

            rows = eliminate(rows)
            for i in range(j + 1, BLOCK):
                cols[i] = eliminate(cols[i])
        new = whole
        for j in range(BLOCK):
            new = new - whole[:, j : j + 1] * rows[j : j + 1, :]
        m_ref[...] = pltpu.roll(new, width - BLOCK, 1)
        m_ref[pl.ds(start, BLOCK), :] = pltpu.roll(rows, width - BLOCK, 1)
        return carry

    lax.fori_loop(0, order // BLOCK, block, 0)


def step_kernel(
    groups,
    slabs,
    count_ref,
    off_hbm,
    obs_hbm,
    noise_hbm,
    pert_hbm,
    fields_ref,
    vel_ref,
    dif_ref,
    ret,
    off_ref,
    obs_ref,
    noise_ref,
    pert_ref,
    bt,
    a2,
    both,
    high,
    v_ref,
    w_ref,
    ext,
    velx,
    difx,
    mid,
    every,
    xs,
    rhs,
    means,
    acc,
    pair,
    sums,
    m_ref,
    local_sem,
    halo_send,
    halo_recv,
    es_sem,
    er_sem,
    ss_sem,
    sr_sem,
):
    g, s = lax.axis_index("grp"), lax.axis_index("slab")
    members, planes, ys, xsz = fields_ref.shape
    order = members * groups
    last = planes + STEPS

    loads = [
        pltpu.make_async_copy(source, target, local_sem.at[i])
        for i, (source, target) in enumerate(
            (
                (off_hbm, off_ref),
                (noise_hbm, noise_ref),
                (obs_hbm, obs_ref),
                (pert_hbm, pert_ref),
                (fields_ref, ext.at[:, 2:last]),
                (vel_ref, velx.at[:, 1 : planes + 1]),
                (dif_ref, difx.at[1 : planes + 1]),
            )
        )
    ]
    for copy in loads[4:] + loads[:4]:
        copy.start()

    def group_peer(r):
        return (lax.rem(g + r, groups), s)

    def slab_peer(r):
        return (g, lax.rem(s + r, slabs))

    barrier = pltpu.get_barrier_semaphore()
    for r in range(1, slabs):
        pl.semaphore_signal(barrier, inc=1, device_id=slab_peer(r), device_id_type=MESH)
    for r in range(1, groups):
        pl.semaphore_signal(barrier, inc=1, device_id=group_peer(r), device_id_type=MESH)

    def coefficients(p):
        courant = [velx[c, p].astype(jnp.float32)[None] * COURANT for c in range(3)]
        return courant + [difx[p][None]]

    def first_step(p, carry):
        mid[:, p] = advance(ext[:, p], ext[:, p + 1], ext[:, p + 2], *coefficients(p))
        return carry

    def units(p):
        return pl.ds(p * ys, ys)

    square = groups == 4
    beside = g + 1 - 2 * lax.rem(g, 2)
    above = lax.rem(g + 2, groups)

    def block_copy(kind, p, block, peer):
        return pltpu.make_async_remote_copy(
            src_ref=every.at[units(p), block],
            dst_ref=every.at[units(p), block],
            send_sem=es_sem.at[kind, p],
            recv_sem=er_sem.at[kind, p],
            device_id=(peer, s),
            device_id_type=MESH,
        )

    def own_copies(p):
        if square:
            return [block_copy(1, p, g, beside), block_copy(2, p, g, above)]
        return [block_copy(r, p, g, lax.rem(g + r, groups)) for r in range(1, groups)]

    def forward_copy(p):
        turn = lax.rem(p, 2)
        block = beside + (above - beside) * turn
        return block_copy(3, p, block, above + (beside - above) * turn)

    def forward(p):
        if square:
            block_copy(1 + lax.rem(p, 2), p, g, beside).wait_recv()
            forward_copy(p).start()

    def arrived(p):
        if square:
            block_copy(2 - lax.rem(p, 2), p, g, beside).wait_recv()
            block_copy(3, p, g, beside).wait_recv()
        else:
            for copy in own_copies(p):
                copy.wait_recv()

    def second_step(p, carry):
        res = advance(mid[:, p], mid[:, p + 1], mid[:, p + 2], *coefficients(p + 1))
        every[units(p), g] = jnp.swapaxes(res, 0, 1)
        for copy in own_copies(p):
            copy.start()
        return carry

    for copy in loads[4:]:
        copy.wait()
    lax.fori_loop(2, planes, first_step, 0)
    pl.semaphore_wait(barrier, slabs + groups - 2)

    def halo(sign, k, src, dst):
        return pltpu.make_async_remote_copy(
            src_ref=src,
            dst_ref=dst,
            send_sem=halo_send.at[(sign + 1) // 2, k],
            recv_sem=halo_recv.at[(sign + 1) // 2, k],
            device_id=(g, lax.rem(s + sign + slabs, slabs)),
            device_id_type=MESH,
        )

    up = [
        halo(1, 0, fields_ref.at[:, planes - 2 : planes], ext.at[:, 0:2]),
        halo(1, 1, vel_ref.at[:, planes - 1 : planes], velx.at[:, 0:1]),
        halo(1, 2, dif_ref.at[planes - 1 : planes], difx.at[0:1]),
    ]
    down = [
        halo(-1, 0, fields_ref.at[:, 0:2], ext.at[:, last : last + 2]),
        halo(-1, 1, vel_ref.at[:, 0:1], velx.at[:, planes + 1 : planes + 2]),
        halo(-1, 2, dif_ref.at[0:1], difx.at[planes + 1 : planes + 2]),
    ]

    @pl.when(s < slabs - 1)
    def _():
        for copy in up:
            copy.start()

    @pl.when(s > 0)
    def _():
        for copy in down:
            copy.start()

    lax.fori_loop(2, planes - 2, second_step, 0)

    for copy in loads[0:4]:
        copy.wait()
    slots = off_ref.shape[1]
    low = off_ref[...] % bt.shape[0]
    high_row = off_ref[...] // bt.shape[0]
    spread_low(bt, jnp.broadcast_to(low.astype(jnp.float32), (TILE, slots)).astype(jnp.bfloat16))

    @pl.when(s == 0)
    def _():
        ext[:, 0:2] = jnp.zeros((members, 2, ys, xsz), jnp.float32)
        velx[:, 0:1] = jnp.zeros((3, 1, ys, xsz), jnp.int32)
        difx[0:1] = jnp.zeros((1, ys, xsz), jnp.float32)

    @pl.when(s == slabs - 1)
    def _():
        ext[:, last : last + 2] = jnp.zeros((members, 2, ys, xsz), jnp.float32)
        velx[:, planes + 1 : planes + 2] = jnp.zeros((3, 1, ys, xsz), jnp.int32)
        difx[planes + 1 : planes + 2] = jnp.zeros((1, ys, xsz), jnp.float32)

    @pl.when(s > 0)
    def _():
        for copy in up:
            copy.wait_recv()

    @pl.when(s < slabs - 1)
    def _():
        for copy in down:
            copy.wait_recv()

    lax.fori_loop(0, 2, first_step, 0)
    lax.fori_loop(planes, planes + 2, first_step, 0)

    @pl.when(s == 0)
    def _():
        mid[:, 0] = jnp.zeros((members, ys, xsz), jnp.float32)

    @pl.when(s == slabs - 1)
    def _():
        mid[:, planes + 1] = jnp.zeros((members, ys, xsz), jnp.float32)

    lax.fori_loop(planes - 2, planes, second_step, 0)
    lax.fori_loop(0, 2, second_step, 0)
    turns = [(i + 2) % planes for i in range(planes)]
    for p in turns[:3]:
        forward(p)

    noise = noise_ref[...]
    slot = lax.broadcasted_iota(jnp.int32, noise.shape, 1)
    inverse = jnp.where(slot < count_ref[0], 1.0 / noise, 0.0)
    first, second = split_two((obs_ref[...] / noise + pert_ref[...]) * inverse)
    both[0:members, :] = first.astype(jnp.bfloat16)
    both[members : 2 * members, :] = second.astype(jnp.bfloat16)
    high[...] = jnp.broadcast_to(high_row.astype(jnp.float32), (TILE, slots)).astype(jnp.bfloat16)
    scatter_weights(high_row, inverse * inverse, bt, w_ref)
    forward(turns[3])

    per = planes * ys // PIECES

    def scatter_turn(q):

        def store(u, value):
            v_ref[q * per + u] = value

        scatter_group(jnp.int32(q), high, both, bt, a2, store)

    scatter_turn(0)
    for p in turns[4:]:
        forward(p)
    scatter_turn(1)

    ratio = w_ref.shape[0]
    total_rows = order + members
    acc[...] = jnp.zeros(acc.shape, jnp.float32)

    def plane_sums(i, carry):
        p = lax.rem(i + 2, planes)
        arrived(p)
        base = p * ys * xsz
        for u in range(ys):
            unit = p * ys + u
            x = every[unit].reshape(order, xsz)
            mean = jnp.sum(x, axis=0, keepdims=True) / order
            w = w_ref[u % ratio, pl.ds(p * (ys // ratio) + u // ratio, 1), :]
            means[pl.ds(unit, 1), :] = mean
            mine = every[unit, g]
            centered = x - mean
            first, second = split_two(centered)
            upper, lower = split_two(
                jnp.concatenate([centered * w, v_ref[unit] - mine * w], axis=0)
            )
            lanes = pl.ds(pl.multiple_of(base + u * xsz, xsz), xsz)
            xs[0:order, lanes] = first.astype(jnp.bfloat16)
            xs[order : 2 * order, lanes] = second.astype(jnp.bfloat16)
            rhs[0:total_rows, u * xsz : (u + 1) * xsz] = upper.astype(jnp.bfloat16)
            rhs[total_rows:, u * xsz : (u + 1) * xsz] = lower.astype(jnp.bfloat16)
        acc[...] += lax.dot_general(
            rhs[...],
            xs[:, pl.ds(pl.multiple_of(base, ys * xsz), ys * xsz)],
            NT,
            preferred_element_type=jnp.float32,
        )
        return carry

    lax.fori_loop(0, planes, plane_sums, 0)

    mine = (acc[0:total_rows] + acc[total_rows:]) / (order - 1)
    mine = mine[:, 0:order] + mine[:, order:]
    pieces = [mine[0:order], mine[order:]]
    folds = 2 if order < LANES else 1
    if folds == 2:
        pieces = [
            jnp.concatenate([a[: a.shape[0] // 2], a[a.shape[0] // 2 :]], axis=1) for a in pieces
        ]
    core, z = lax.rem(s, 2), lax.div(s, 2)
    heights = slabs // 2
    pair[core] = jnp.concatenate(pieces, axis=0)

    def sum_copy(ref, place, sem, r, peer):
        return pltpu.make_async_remote_copy(
            src_ref=ref.at[place],
            dst_ref=ref.at[place],
            send_sem=sem[0].at[r],
            recv_sem=sem[1].at[r],
            device_id=(g, peer),
            device_id_type=MESH,
        )

    pair_copy = sum_copy(pair, core, (ss_sem, sr_sem), 0, s + 1 - 2 * core)
    pair_copy.start()
    pair_copy.wait_recv()
    sums[z] = pair[0] + pair[1]
    s_copies = [
        sum_copy(sums, z, (ss_sem, sr_sem), r, lax.rem(z + r, heights) * 2 + core)
        for r in range(1, heights)
    ]
    for copy in s_copies:
        copy.start()
    for copy in s_copies:
        copy.wait_recv()
    added = sums[0]
    for i in range(1, heights):
        added = added + sums[i]

    width = m_ref.shape[1]
    gram, cross = added[0 : order // folds], added[order // folds :]
    if folds == 2:
        gram, cross = [
            jnp.concatenate([a[:, 0:order], a[:, order:]], axis=0) for a in (gram, cross)
        ]
    diagonal = lax.broadcasted_iota(jnp.int32, gram.shape, 0) == lax.broadcasted_iota(
        jnp.int32, gram.shape, 1
    )
    spare = jnp.zeros((width - order - members, order), jnp.float32)
    cross = jnp.concatenate([cross, spare], axis=0).T
    m_ref[...] = jnp.concatenate([gram + jnp.where(diagonal, 1.0, 0.0), cross], axis=1)
    solve_in_place(m_ref)

    weights = m_ref[...].T[0:members]
    total = jnp.sum(weights, axis=1, keepdims=True)
    left = jnp.concatenate(
        [jnp.concatenate([half, half], axis=1) for half in split_two(weights)], axis=0
    ).astype(jnp.bfloat16)

    def plane_update(p, carry):
        lanes = pl.ds(pl.multiple_of(p * ys * xsz, ys * xsz), ys * xsz)
        res = lax.dot_general(left, xs[:, lanes], NN, preferred_element_type=jnp.float32)
        res = res[0:members] + res[members:]
        new = [
            every[p * ys + u, g]
            + (res[:, u * xsz : (u + 1) * xsz] + total * means[pl.ds(p * ys + u, 1), :])
            for u in range(ys)
        ]
        ret[:, p] = jnp.swapaxes(jnp.stack(new, axis=0), 0, 1)
        return carry

    lax.fori_loop(0, planes, plane_update, 0)

    def sent_plane(p, carry):
        for copy in own_copies(p):
            copy.wait_send()
        if square:
            forward_copy(p).wait_send()
        return carry

    lax.fori_loop(0, planes, sent_plane, 0)
    for copy in [pair_copy] + s_copies:
        copy.wait_send()

    @pl.when(s < slabs - 1)
    def _():
        for copy in up:
            copy.wait_send()

    @pl.when(s > 0)
    def _():
        for copy in down:
            copy.wait_send()


def finish_kernel(ret, out_hbm, sem):
    copy = pltpu.make_async_copy(ret, out_hbm, sem)
    copy.start()
    copy.wait()


def local(
    groups,
    slabs,
    fields,
    velocity,
    diffusivity,
    sensor_offsets,
    sensor_counts,
    observations,
    noise_scale,
    perturbation,
):
    members, planes, ys, xsz = fields.shape
    units = planes * ys
    order = members * groups
    slots = sensor_offsets.shape[0]
    low = 2 * LANES
    highs = units * xsz // low
    width = -(-(order + members) // LANES) * LANES
    folds = 2 if order < LANES else 1
    folded = ((order + members) // folds, order * folds)
    vmem = pl.BlockSpec(memory_space=pltpu.VMEM)
    f32 = jnp.float32
    scratch = [
        pltpu.VMEM((1, slots), jnp.int32),
        pltpu.VMEM((1, slots), f32),
        pltpu.VMEM((1, slots), f32),
        pltpu.VMEM((members, slots), f32),
        pltpu.VMEM((low, slots), jnp.bfloat16),
        pltpu.VMEM((highs // PIECES * 2 * members, slots), jnp.bfloat16),
        pltpu.VMEM((2 * members, slots), jnp.bfloat16),
        pltpu.VMEM((TILE, slots), jnp.bfloat16),
        pltpu.VMEM((units, members, xsz), f32),
        pltpu.VMEM((low // LANES, highs, LANES), f32),
        pltpu.VMEM((members, planes + 4, ys, xsz), f32),
        pltpu.VMEM((3, planes + 2, ys, xsz), jnp.int32),
        pltpu.VMEM((planes + 2, ys, xsz), f32),
        pltpu.VMEM((members, planes + 2, ys, xsz), f32),
        pltpu.VMEM((units, groups, members, xsz), f32),
        pltpu.VMEM((2 * order, units * xsz), jnp.bfloat16),
        pltpu.VMEM((2 * (order + members), ys * xsz), jnp.bfloat16),
        pltpu.VMEM((units, xsz), f32),
        pltpu.VMEM((2 * (order + members), 2 * order), f32),
        pltpu.VMEM((2,) + folded, f32),
        pltpu.VMEM((slabs // 2,) + folded, f32),
        pltpu.VMEM((order, width), f32),
        pltpu.SemaphoreType.DMA((7,)),
        pltpu.SemaphoreType.DMA((2, 3)),
        pltpu.SemaphoreType.DMA((2, 3)),
        pltpu.SemaphoreType.DMA((groups, planes)),
        pltpu.SemaphoreType.DMA((groups, planes)),
        pltpu.SemaphoreType.DMA((slabs // 2,)),
        pltpu.SemaphoreType.DMA((slabs // 2,)),
    ]
    hbm = pl.BlockSpec(memory_space=pltpu.HBM)
    ret = pl.pallas_call(
        functools.partial(step_kernel, groups, slabs),
        out_shape=pltpu.VMEM(fields.shape, f32),
        in_specs=[pl.BlockSpec(memory_space=pltpu.SMEM)] + [hbm] * 7,
        out_specs=vmem,
        scratch_shapes=scratch,
        compiler_params=pltpu.CompilerParams(
            collective_id=0, has_side_effects=True, vmem_limit_bytes=56 * 1024 * 1024
        ),
        name="ensemble_step",
    )(
        sensor_counts,
        sensor_offsets[None],
        observations[None],
        noise_scale[None],
        perturbation,
        fields,
        velocity,
        diffusivity,
    )
    return pl.pallas_call(
        finish_kernel,
        out_shape=jax.ShapeDtypeStruct(fields.shape, f32),
        in_specs=[vmem],
        out_specs=hbm,
        scratch_shapes=[pltpu.SemaphoreType.DMA],
        compiler_params=pltpu.CompilerParams(vmem_limit_bytes=4 * 1024 * 1024),
        name="finish",
    )(ret)


def solution(mesh):
    return jax.shard_map(
        functools.partial(local, mesh.shape["grp"], mesh.shape["slab"]),
        mesh=mesh,
        in_specs=(
            P("grp", "slab", None, None),
            P(None, "slab", None, None),
            P("slab", None, None),
            P("slab"),
            P("slab"),
            P("slab"),
            P("slab"),
            P("grp", "slab"),
        ),
        out_specs=P("grp", "slab", None, None),
        check_vma=False,
    )
```

```python
import functools
import math

import jax
import jax.numpy as jnp
from jax import lax
from jax.experimental import pallas as pl
from jax.experimental.pallas import tpu as pltpu
from jax.sharding import PartitionSpec as P

STEPS = 2
COURANT = 0.12
PIECES = 4
TILE = 16
LANES = 128
BLOCK = 8
MESH = pl.DeviceIdType.MESH
NT = (((1,), (1,)), ((), ()))
NN = (((1,), (0,)), ((), ()))


def split_two(values):
    high = values.astype(jnp.bfloat16).astype(jnp.float32)
    return high, values - high


def spread_low(bt, low):
    rows = lax.broadcasted_iota(jnp.int32, low.shape, 0).astype(jnp.float32)
    one, zero = jnp.bfloat16(1.0), jnp.bfloat16(0.0)
    for r in range(0, bt.shape[0], TILE):
        wanted = (rows + r).astype(jnp.bfloat16)
        bt[r : r + TILE, :] = jnp.where(low == wanted, one, zero)


def scatter_group(q, high, both, bt, a2, store):
    rows = both.shape[0]
    members = rows // 2
    per_group = a2.shape[0] // rows
    ratio = bt.shape[0] // LANES
    zero = jnp.bfloat16(0.0)
    for k in range(per_group):
        wanted = (q * per_group + k).astype(jnp.float32).astype(jnp.bfloat16)
        for t in range(0, rows, TILE):
            a2[k * rows + t : k * rows + t + TILE, :] = jnp.where(
                high[...] == wanted, both[t : t + TILE, :], zero
            )
    res = lax.dot_general(a2[...], bt[...], NT, preferred_element_type=jnp.float32)
    for k in range(per_group):
        start = k * rows
        added = res[start : start + members] + res[start + members : start + rows]
        for i in range(ratio):
            store(k * ratio + i, added[:, i * LANES : (i + 1) * LANES])


def scatter_weights(high, weight, bt, w_ref):
    rows = w_ref.shape[1]
    wanted = lax.broadcasted_iota(jnp.int32, (rows, high.shape[1]), 0)
    first, second = split_two(jnp.where(wanted == high, weight, 0.0))
    stacked = jnp.concatenate([first, second], axis=0).astype(jnp.bfloat16)
    res = lax.dot_general(stacked, bt[...], NT, preferred_element_type=jnp.float32)
    total = res[:rows] + res[rows:]
    for i in range(w_ref.shape[0]):
        w_ref[i] = total[:, i * LANES : (i + 1) * LANES]


def upwind(courant, center, lower_side, upper_side):
    return jnp.maximum(courant, 0.0) * (center - lower_side) + jnp.minimum(courant, 0.0) * (
        upper_side - center
    )


def advance(below, center, above, cz, cy, cx, diffusivity):
    y_size, x_size = center.shape[1:]
    south = pltpu.roll(center, 1, 1)
    north = pltpu.roll(center, y_size - 1, 1)
    west = pltpu.roll(center, 1, 2)
    east = pltpu.roll(center, x_size - 1, 2)
    transport = upwind(cz, center, below, above) + upwind(cy, center, south, north)
    transport = transport + upwind(cx, center, west, east)
    laplace = below + above + south + north + west + east - 6.0 * center
    return center - transport + diffusivity * laplace


def solve_in_place(m_ref):
    order, width = m_ref.shape

    def block(b, carry):
        start = pl.multiple_of(b * BLOCK, BLOCK)
        whole = m_ref[...]
        rows = m_ref[pl.ds(start, BLOCK), :]
        row_id = lax.broadcasted_iota(jnp.int32, (BLOCK, width), 0)
        cols = [jnp.broadcast_to(rows[:, i : i + 1], (BLOCK, width)) for i in range(BLOCK)]
        for j in range(BLOCK):
            inverse = 1.0 / cols[j][j : j + 1, :]
            mine = cols[j]
            here = row_id == j

            def eliminate(t):
                pivot_row = t[j : j + 1, :] * inverse
                return jnp.where(here, pivot_row, t - mine * pivot_row)

            rows = eliminate(rows)
            for i in range(j + 1, BLOCK):
                cols[i] = eliminate(cols[i])
        new = whole
        for j in range(BLOCK):
            new = new - whole[:, j : j + 1] * rows[j : j + 1, :]
        m_ref[...] = pltpu.roll(new, width - BLOCK, 1)
        m_ref[pl.ds(start, BLOCK), :] = pltpu.roll(rows, width - BLOCK, 1)
        return carry

    lax.fori_loop(0, order // BLOCK, block, 0)


def step_kernel(
    groups,
    slabs,
    count_ref,
    off_hbm,
    obs_hbm,
    noise_hbm,
    pert_hbm,
    fields_ref,
    vel_ref,
    dif_ref,
    ret,
    xs,
    means,
    left,
    total,
    off_ref,
    obs_ref,
    noise_ref,
    pert_ref,
    bt,
    a2,
    both,
    high,
    v_ref,
    w_ref,
    ext,
    velx,
    difx,
    mid,
    every,
    rhs,
    acc,
    pair,
    sums,
    m_ref,
    local_sem,
    halo_send,
    halo_recv,
    es_sem,
    er_sem,
    ss_sem,
    sr_sem,
):
    g, s = lax.axis_index("grp"), lax.axis_index("slab")
    members, planes, ys, xsz = fields_ref.shape
    order = members * groups
    last = planes + STEPS

    loads = [
        pltpu.make_async_copy(source, target, local_sem.at[i])
        for i, (source, target) in enumerate(
            (
                (off_hbm, off_ref),
                (noise_hbm, noise_ref),
                (obs_hbm, obs_ref),
                (pert_hbm, pert_ref),
                (fields_ref, ext.at[:, 2:last]),
                (vel_ref, velx.at[:, 1 : planes + 1]),
                (dif_ref, difx.at[1 : planes + 1]),
            )
        )
    ]
    for copy in loads[4:] + loads[:4]:
        copy.start()

    def group_peer(r):
        return (lax.rem(g + r, groups), s)

    def slab_peer(r):
        return (g, lax.rem(s + r, slabs))

    barrier = pltpu.get_barrier_semaphore()
    for r in range(1, slabs):
        pl.semaphore_signal(barrier, inc=1, device_id=slab_peer(r), device_id_type=MESH)
    for r in range(1, groups):
        pl.semaphore_signal(barrier, inc=1, device_id=group_peer(r), device_id_type=MESH)

    def coefficients(p):
        courant = [velx[c, p].astype(jnp.float32)[None] * COURANT for c in range(3)]
        return courant + [difx[p][None]]

    def first_step(p, carry):
        mid[:, p] = advance(ext[:, p], ext[:, p + 1], ext[:, p + 2], *coefficients(p))
        return carry

    def units(p):
        return pl.ds(p * ys, ys)

    square = groups == 4
    beside = g + 1 - 2 * lax.rem(g, 2)
    above = lax.rem(g + 2, groups)

    def block_copy(kind, p, block, peer):
        return pltpu.make_async_remote_copy(
            src_ref=every.at[units(p), block],
            dst_ref=every.at[units(p), block],
            send_sem=es_sem.at[kind, p],
            recv_sem=er_sem.at[kind, p],
            device_id=(peer, s),
            device_id_type=MESH,
        )

    def own_copies(p):
        if square:
            return [block_copy(1, p, g, beside), block_copy(2, p, g, above)]
        return [block_copy(r, p, g, lax.rem(g + r, groups)) for r in range(1, groups)]

    def forward_copy(p):
        turn = lax.rem(p, 2)
        block = beside + (above - beside) * turn
        return block_copy(3, p, block, above + (beside - above) * turn)

    def forward(p):
        if square:
            block_copy(1 + lax.rem(p, 2), p, g, beside).wait_recv()
            forward_copy(p).start()

    def arrived(p):
        if square:
            block_copy(2 - lax.rem(p, 2), p, g, beside).wait_recv()
            block_copy(3, p, g, beside).wait_recv()
        else:
            for copy in own_copies(p):
                copy.wait_recv()

    def second_step(p, carry):
        res = advance(mid[:, p], mid[:, p + 1], mid[:, p + 2], *coefficients(p + 1))
        every[units(p), g] = jnp.swapaxes(res, 0, 1)
        ret[:, p] = res
        return carry

    def inner_step(p, carry):
        second_step(p, carry)
        for copy in own_copies(p):
            copy.start()
        return carry

    for copy in loads[4:]:
        copy.wait()
    lax.fori_loop(2, planes, first_step, 0)
    pl.semaphore_wait(barrier, slabs + groups - 2)

    def halo(sign, k, src, dst):
        return pltpu.make_async_remote_copy(
            src_ref=src,
            dst_ref=dst,
            send_sem=halo_send.at[(sign + 1) // 2, k],
            recv_sem=halo_recv.at[(sign + 1) // 2, k],
            device_id=(g, lax.rem(s + sign + slabs, slabs)),
            device_id_type=MESH,
        )

    up = [
        halo(1, 0, fields_ref.at[:, planes - 2 : planes], ext.at[:, 0:2]),
        halo(1, 1, vel_ref.at[:, planes - 1 : planes], velx.at[:, 0:1]),
        halo(1, 2, dif_ref.at[planes - 1 : planes], difx.at[0:1]),
    ]
    down = [
        halo(-1, 0, fields_ref.at[:, 0:2], ext.at[:, last : last + 2]),
        halo(-1, 1, vel_ref.at[:, 0:1], velx.at[:, planes + 1 : planes + 2]),
        halo(-1, 2, dif_ref.at[0:1], difx.at[planes + 1 : planes + 2]),
    ]

    @pl.when(s < slabs - 1)
    def _():
        for copy in up:
            copy.start()

    @pl.when(s > 0)
    def _():
        for copy in down:
            copy.start()

    lax.fori_loop(2, planes - 2, inner_step, 0)

    for copy in loads[0:4]:
        copy.wait()
    slots = off_ref.shape[1]
    low = off_ref[...] % bt.shape[0]
    high_row = off_ref[...] // bt.shape[0]
    spread_low(bt, jnp.broadcast_to(low.astype(jnp.float32), (TILE, slots)).astype(jnp.bfloat16))

    noise = noise_ref[...]
    slot = lax.broadcasted_iota(jnp.int32, noise.shape, 1)
    inverse = jnp.where(slot < count_ref[0], 1.0 / noise, 0.0)
    first, second = split_two((obs_ref[...] / noise + pert_ref[...]) * inverse)
    both[0:members, :] = first.astype(jnp.bfloat16)
    both[members : 2 * members, :] = second.astype(jnp.bfloat16)
    high[...] = jnp.broadcast_to(high_row.astype(jnp.float32), (TILE, slots)).astype(jnp.bfloat16)
    scatter_weights(high_row, inverse * inverse, bt, w_ref)
    @pl.when(s == 0)
    def _():
        ext[:, 0:2] = jnp.zeros((members, 2, ys, xsz), jnp.float32)
        velx[:, 0:1] = jnp.zeros((3, 1, ys, xsz), jnp.int32)
        difx[0:1] = jnp.zeros((1, ys, xsz), jnp.float32)

    @pl.when(s == slabs - 1)
    def _():
        ext[:, last : last + 2] = jnp.zeros((members, 2, ys, xsz), jnp.float32)
        velx[:, planes + 1 : planes + 2] = jnp.zeros((3, 1, ys, xsz), jnp.int32)
        difx[planes + 1 : planes + 2] = jnp.zeros((1, ys, xsz), jnp.float32)

    @pl.when(s > 0)
    def _():
        for copy in up:
            copy.wait_recv()

    @pl.when(s < slabs - 1)
    def _():
        for copy in down:
            copy.wait_recv()

    lax.fori_loop(0, 2, first_step, 0)
    lax.fori_loop(planes, planes + 2, first_step, 0)

    @pl.when(s == 0)
    def _():
        mid[:, 0] = jnp.zeros((members, ys, xsz), jnp.float32)

    @pl.when(s == slabs - 1)
    def _():
        mid[:, planes + 1] = jnp.zeros((members, ys, xsz), jnp.float32)

    lax.fori_loop(planes - 2, planes, second_step, 0)
    lax.fori_loop(0, 2, second_step, 0)
    edges = [planes - 2, planes - 1, 0, 1]
    if square:
        for p, q in zip(edges[0::2] + edges[1::2], edges[1::2] + edges[0::2]):
            block_copy(1, p, g, beside).start()
            block_copy(2, q, g, above).start()
    else:
        for p in edges:
            for copy in own_copies(p):
                copy.start()

    per = planes * ys // PIECES

    def scatter_turn(q):

        def store(u, value):
            v_ref[q * per + u] = value

        scatter_group(jnp.int32(q), high, both, bt, a2, store)

    forward(2)
    for q in range(PIECES):
        if q < planes - 5:
            forward(q + 3)
        scatter_turn(q)
    for p in edges:
        forward(p)

    ratio = w_ref.shape[0]
    total_rows = order + members
    acc[...] = jnp.zeros(acc.shape, jnp.float32)

    def plane_sums(i, carry):
        p = lax.rem(i + 2, planes)
        arrived(p)
        base = p * ys * xsz
        for u in range(ys):
            unit = p * ys + u
            x = every[unit].reshape(order, xsz)
            mean = jnp.sum(x, axis=0, keepdims=True) / order
            w = w_ref[u % ratio, pl.ds(p * (ys // ratio) + u // ratio, 1), :]
            means[pl.ds(unit, 1), :] = mean
            mine = every[unit, g]
            centered = x - mean
            first, second = split_two(centered)
            upper, lower = split_two(
                jnp.concatenate([centered * w, v_ref[unit] - mine * w], axis=0)
            )
            lanes = pl.ds(pl.multiple_of(base + u * xsz, xsz), xsz)
            xs[0:order, lanes] = first.astype(jnp.bfloat16)
            xs[order : 2 * order, lanes] = second.astype(jnp.bfloat16)
            rhs[0:total_rows, u * xsz : (u + 1) * xsz] = upper.astype(jnp.bfloat16)
            rhs[total_rows:, u * xsz : (u + 1) * xsz] = lower.astype(jnp.bfloat16)
        acc[...] += lax.dot_general(
            rhs[...],
            xs[:, pl.ds(pl.multiple_of(base, ys * xsz), ys * xsz)],
            NT,
            preferred_element_type=jnp.float32,
        )
        return carry

    lax.fori_loop(0, planes, plane_sums, 0)

    mine = (acc[0:total_rows] + acc[total_rows:]) / (order - 1)
    mine = mine[:, 0:order] + mine[:, order:]
    pieces = [mine[0:order], mine[order:]]
    folds = 2 if order < LANES else 1
    if folds == 2:
        pieces = [
            jnp.concatenate([a[: a.shape[0] // 2], a[a.shape[0] // 2 :]], axis=1) for a in pieces
        ]
    core, z = lax.rem(s, 2), lax.div(s, 2)
    heights = slabs // 2
    pair[core] = jnp.concatenate(pieces, axis=0)

    def sum_copy(ref, place, sem, r, peer):
        return pltpu.make_async_remote_copy(
            src_ref=ref.at[place],
            dst_ref=ref.at[place],
            send_sem=sem[0].at[r],
            recv_sem=sem[1].at[r],
            device_id=(g, peer),
            device_id_type=MESH,
        )

    pair_copy = sum_copy(pair, core, (ss_sem, sr_sem), 0, s + 1 - 2 * core)
    pair_copy.start()
    pair_copy.wait_recv()
    sums[z] = pair[0] + pair[1]
    s_copies = [
        sum_copy(sums, z, (ss_sem, sr_sem), r, lax.rem(z + r, heights) * 2 + core)
        for r in range(1, heights)
    ]
    for copy in s_copies:
        copy.start()

    def sent_plane(p, carry):
        for copy in own_copies(p):
            copy.wait_send()
        if square:
            forward_copy(p).wait_send()
        return carry

    lax.fori_loop(0, planes, sent_plane, 0)
    pair_copy.wait_send()

    @pl.when(s < slabs - 1)
    def _():
        for copy in up:
            copy.wait_send()

    @pl.when(s > 0)
    def _():
        for copy in down:
            copy.wait_send()

    for copy in s_copies:
        copy.wait()
    added = sums[0]
    for i in range(1, heights):
        added = added + sums[i]

    width = m_ref.shape[1]
    gram, cross = added[0 : order // folds], added[order // folds :]
    if folds == 2:
        gram, cross = [
            jnp.concatenate([a[:, 0:order], a[:, order:]], axis=0) for a in (gram, cross)
        ]
    diagonal = lax.broadcasted_iota(jnp.int32, gram.shape, 0) == lax.broadcasted_iota(
        jnp.int32, gram.shape, 1
    )
    spare = jnp.zeros((width - order - members, order), jnp.float32)
    cross = jnp.concatenate([cross, spare], axis=0).T
    m_ref[...] = jnp.concatenate([gram + jnp.where(diagonal, 1.0, 0.0), cross], axis=1)
    solve_in_place(m_ref)

    weights = m_ref[...].T[0:members]
    total[...] = jnp.broadcast_to(jnp.sum(weights, axis=1, keepdims=True), total.shape)
    left[...] = jnp.concatenate(
        [jnp.concatenate([half, half], axis=1) for half in split_two(weights)], axis=0
    ).astype(jnp.bfloat16)


def finish_kernel(ret, xs, means, left, total, out_hbm, stage, sem):
    members, planes, ys, xsz = out_hbm.shape
    copies = []
    for p in range(planes):
        lanes = slice(p * ys * xsz, (p + 1) * ys * xsz)
        res = lax.dot_general(
            left[...], xs[:, lanes], NN, preferred_element_type=jnp.float32
        )
        res = res[0:members] + res[members:]
        new = [
            res[:, u * xsz : (u + 1) * xsz] + total[...] * means[p * ys + u : p * ys + u + 1, :]
            for u in range(ys)
        ]
        stage[:, p] = ret[:, p] + jnp.swapaxes(jnp.stack(new, axis=0), 0, 1)
        copies.append(pltpu.make_async_copy(stage.at[:, p], out_hbm.at[:, p], sem.at[p]))
        copies[-1].start()
    for copy in copies:
        copy.wait()


def local(
    groups,
    slabs,
    fields,
    velocity,
    diffusivity,
    sensor_offsets,
    sensor_counts,
    observations,
    noise_scale,
    perturbation,
):
    members, planes, ys, xsz = fields.shape
    units = planes * ys
    order = members * groups
    slots = sensor_offsets.shape[0]
    low = 2 * LANES
    highs = units * xsz // low
    width = -(-(order + members) // LANES) * LANES
    folds = 2 if order < LANES else 1
    folded = ((order + members) // folds, order * folds)
    vmem = pl.BlockSpec(memory_space=pltpu.VMEM)
    f32 = jnp.float32
    scratch = [
        pltpu.VMEM((1, slots), jnp.int32),
        pltpu.VMEM((1, slots), f32),
        pltpu.VMEM((1, slots), f32),
        pltpu.VMEM((members, slots), f32),
        pltpu.VMEM((low, slots), jnp.bfloat16),
        pltpu.VMEM((highs // PIECES * 2 * members, slots), jnp.bfloat16),
        pltpu.VMEM((2 * members, slots), jnp.bfloat16),
        pltpu.VMEM((TILE, slots), jnp.bfloat16),
        pltpu.VMEM((units, members, xsz), f32),
        pltpu.VMEM((low // LANES, highs, LANES), f32),
        pltpu.VMEM((members, planes + 4, ys, xsz), f32),
        pltpu.VMEM((3, planes + 2, ys, xsz), jnp.int32),
        pltpu.VMEM((planes + 2, ys, xsz), f32),
        pltpu.VMEM((members, planes + 2, ys, xsz), f32),
        pltpu.VMEM((units, groups, members, xsz), f32),
        pltpu.VMEM((2 * (order + members), ys * xsz), jnp.bfloat16),
        pltpu.VMEM((2 * (order + members), 2 * order), f32),
        pltpu.VMEM((2,) + folded, f32),
        pltpu.VMEM((slabs // 2,) + folded, f32),
        pltpu.VMEM((order, width), f32),
        pltpu.SemaphoreType.DMA((7,)),
        pltpu.SemaphoreType.DMA((2, 3)),
        pltpu.SemaphoreType.DMA((2, 3)),
        pltpu.SemaphoreType.DMA((groups, planes)),
        pltpu.SemaphoreType.DMA((groups, planes)),
        pltpu.SemaphoreType.DMA((slabs // 2,)),
        pltpu.SemaphoreType.DMA((slabs // 2,)),
    ]
    hbm = pl.BlockSpec(memory_space=pltpu.HBM)
    results = [
        pltpu.VMEM(fields.shape, f32),
        pltpu.VMEM((2 * order, units * xsz), jnp.bfloat16),
        pltpu.VMEM((units, xsz), f32),
        pltpu.VMEM((2 * members, 2 * order), jnp.bfloat16),
        pltpu.VMEM((members, xsz), f32),
    ]
    held = sum(math.prod(r.shape) * jnp.dtype(r.dtype).itemsize for r in results)
    room = 58 * 1024 * 1024 - held
    results = pl.pallas_call(
        functools.partial(step_kernel, groups, slabs),
        out_shape=results,
        in_specs=[pl.BlockSpec(memory_space=pltpu.SMEM)] + [hbm] * 7,
        out_specs=[vmem] * len(results),
        scratch_shapes=scratch,
        compiler_params=pltpu.CompilerParams(
            collective_id=0, has_side_effects=True, vmem_limit_bytes=room
        ),
        name="ensemble_step",
    )(
        sensor_counts,
        sensor_offsets[None],
        observations[None],
        noise_scale[None],
        perturbation,
        fields,
        velocity,
        diffusivity,
    )
    return pl.pallas_call(
        finish_kernel,
        out_shape=jax.ShapeDtypeStruct(fields.shape, f32),
        in_specs=[vmem] * len(results),
        out_specs=hbm,
        scratch_shapes=[
            pltpu.VMEM(fields.shape, f32),
            pltpu.SemaphoreType.DMA((planes,)),
        ],
        compiler_params=pltpu.CompilerParams(vmem_limit_bytes=16 * 1024 * 1024),
        name="finish",
    )(*results)


def solution(mesh):
    return jax.shard_map(
        functools.partial(local, mesh.shape["grp"], mesh.shape["slab"]),
        mesh=mesh,
        in_specs=(
            P("grp", "slab", None, None),
            P(None, "slab", None, None),
            P("slab", None, None),
            P("slab"),
            P("slab"),
            P("slab"),
            P("slab"),
            P("grp", "slab"),
        ),
        out_specs=P("grp", "slab", None, None),
        check_vma=False,
    )
```

```python
import functools
import math

import jax
import jax.numpy as jnp
from jax import lax
from jax.experimental import pallas as pl
from jax.experimental.pallas import tpu as pltpu
from jax.sharding import PartitionSpec as P

STEPS = 2
COURANT = 0.12
PIECES = 4
TILE = 16
LANES = 128
BLOCK = 8
MESH = pl.DeviceIdType.MESH
NT = (((1,), (1,)), ((), ()))
NN = (((1,), (0,)), ((), ()))


def split_two(values):
    high = values.astype(jnp.bfloat16).astype(jnp.float32)
    return high, values - high


def spread_low(bt, low):
    rows = lax.broadcasted_iota(jnp.int32, low.shape, 0).astype(jnp.float32)
    one, zero = jnp.bfloat16(1.0), jnp.bfloat16(0.0)
    for r in range(0, bt.shape[0], TILE):
        wanted = (rows + r).astype(jnp.bfloat16)
        bt[r : r + TILE, :] = jnp.where(low == wanted, one, zero)


def scatter_group(q, high, both, bt, a2, store):
    rows = both.shape[0]
    members = rows // 2
    per_group = a2.shape[0] // rows
    ratio = bt.shape[0] // LANES
    zero = jnp.bfloat16(0.0)
    for k in range(per_group):
        wanted = (q * per_group + k).astype(jnp.float32).astype(jnp.bfloat16)
        for t in range(0, rows, TILE):
            a2[k * rows + t : k * rows + t + TILE, :] = jnp.where(
                high[...] == wanted, both[t : t + TILE, :], zero
            )
    res = lax.dot_general(a2[...], bt[...], NT, preferred_element_type=jnp.float32)
    for k in range(per_group):
        start = k * rows
        added = res[start : start + members] + res[start + members : start + rows]
        for i in range(ratio):
            store(k * ratio + i, added[:, i * LANES : (i + 1) * LANES])


def scatter_weights(high, weight, bt, w_ref):
    rows = w_ref.shape[1]
    wanted = lax.broadcasted_iota(jnp.int32, (rows, high.shape[1]), 0)
    first, second = split_two(jnp.where(wanted == high, weight, 0.0))
    stacked = jnp.concatenate([first, second], axis=0).astype(jnp.bfloat16)
    res = lax.dot_general(stacked, bt[...], NT, preferred_element_type=jnp.float32)
    total = res[:rows] + res[rows:]
    for i in range(w_ref.shape[0]):
        w_ref[i] = total[:, i * LANES : (i + 1) * LANES]


def upwind(courant, center, lower_side, upper_side):
    return jnp.maximum(courant, 0.0) * (center - lower_side) + jnp.minimum(courant, 0.0) * (
        upper_side - center
    )


def advance(below, center, above, cz, cy, cx, diffusivity):
    y_size, x_size = center.shape[1:]
    south = pltpu.roll(center, 1, 1)
    north = pltpu.roll(center, y_size - 1, 1)
    west = pltpu.roll(center, 1, 2)
    east = pltpu.roll(center, x_size - 1, 2)
    transport = upwind(cz, center, below, above) + upwind(cy, center, south, north)
    transport = transport + upwind(cx, center, west, east)
    laplace = below + above + south + north + west + east - 6.0 * center
    return center - transport + diffusivity * laplace


def solve_in_place(m_ref):
    order, width = m_ref.shape

    def reduced(whole, rows, at):
        row_id = lax.broadcasted_iota(jnp.int32, rows.shape, 0)
        cols = [jnp.broadcast_to(rows[:, at + i : at + i + 1], rows.shape) for i in range(BLOCK)]
        for j in range(0, BLOCK, 2):
            k = j + 1
            left, right = cols[j], cols[k]
            a, b, c, d = left[j:k, :], right[j:k, :], left[k : k + 1, :], right[k : k + 1, :]
            inverse = 1.0 / (a * d - b * c)

            def eliminate(t):
                upper, lower = t[j:k, :], t[k : k + 1, :]
                first = (d * upper - b * lower) * inverse
                second = (a * lower - c * upper) * inverse
                rest = t - left * first - right * second
                return jnp.where(row_id == j, first, jnp.where(row_id == k, second, rest))

            rows = eliminate(rows)
            for i in range(j + 2, BLOCK):
                cols[i] = eliminate(cols[i])
        new = whole
        for j in range(BLOCK):
            new = new - whole[:, at + j : at + j + 1] * rows[j : j + 1, :]
        return new, rows

    if order < LANES:
        whole = m_ref[...]
        for start in range(0, order, BLOCK):
            stop = start + BLOCK
            new, rows = reduced(whole, whole[start:stop], start)
            kept = [new[:start]] if start else []
            kept += [rows] + ([new[stop:]] if stop < order else [])
            whole = jnp.concatenate(kept, axis=0)
        m_ref[...] = pltpu.roll(whole, width - order, 1)
        return

    def block(b, carry):
        start = pl.multiple_of(b * BLOCK, BLOCK)
        new, rows = reduced(m_ref[...], m_ref[pl.ds(start, BLOCK), :], 0)
        m_ref[...] = pltpu.roll(new, width - BLOCK, 1)
        m_ref[pl.ds(start, BLOCK), :] = pltpu.roll(rows, width - BLOCK, 1)
        return carry

    lax.fori_loop(0, order // BLOCK, block, 0)


def step_kernel(
    groups,
    slabs,
    count_ref,
    off_hbm,
    obs_hbm,
    noise_hbm,
    pert_hbm,
    fields_ref,
    vel_ref,
    dif_ref,
    ret,
    xs,
    means,
    left,
    total,
    off_ref,
    obs_ref,
    noise_ref,
    pert_ref,
    bt,
    a2,
    both,
    high,
    v_ref,
    w_ref,
    ext,
    velx,
    difx,
    mid,
    every,
    rhs,
    acc,
    pair,
    sums,
    m_ref,
    local_sem,
    halo_send,
    halo_recv,
    es_sem,
    er_sem,
    ss_sem,
    sr_sem,
):
    g, s = lax.axis_index("grp"), lax.axis_index("slab")
    members, planes, ys, xsz = fields_ref.shape
    order = members * groups
    last = planes + STEPS

    loads = [
        pltpu.make_async_copy(source, target, local_sem.at[i])
        for i, (source, target) in enumerate(
            (
                (off_hbm, off_ref),
                (noise_hbm, noise_ref),
                (obs_hbm, obs_ref),
                (pert_hbm, pert_ref),
                (fields_ref, ext.at[:, 2:last]),
                (vel_ref, velx.at[:, 1 : planes + 1]),
                (dif_ref, difx.at[1 : planes + 1]),
            )
        )
    ]
    for copy in loads[4:] + loads[:4]:
        copy.start()

    def group_peer(r):
        return (lax.rem(g + r, groups), s)

    def slab_peer(r):
        return (g, lax.rem(s + r, slabs))

    barrier = pltpu.get_barrier_semaphore()
    for r in range(1, slabs):
        pl.semaphore_signal(barrier, inc=1, device_id=slab_peer(r), device_id_type=MESH)
    for r in range(1, groups):
        pl.semaphore_signal(barrier, inc=1, device_id=group_peer(r), device_id_type=MESH)

    def coefficients(p):
        courant = [velx[c, p].astype(jnp.float32)[None] * COURANT for c in range(3)]
        return courant + [difx[p][None]]

    def first_step(p, carry):
        mid[:, p] = advance(ext[:, p], ext[:, p + 1], ext[:, p + 2], *coefficients(p))
        return carry

    def units(p):
        return pl.ds(p * ys, ys)

    square = groups == 4
    beside = g + 1 - 2 * lax.rem(g, 2)
    above = lax.rem(g + 2, groups)

    def block_copy(kind, p, block, peer):
        return pltpu.make_async_remote_copy(
            src_ref=every.at[block, units(p)],
            dst_ref=every.at[block, units(p)],
            send_sem=es_sem.at[kind, p],
            recv_sem=er_sem.at[kind, p],
            device_id=(peer, s),
            device_id_type=MESH,
        )

    def own_copies(p):
        if square:
            return [block_copy(1, p, g, beside), block_copy(2, p, g, above)]
        return [block_copy(r, p, g, lax.rem(g + r, groups)) for r in range(1, groups)]

    def forward_copy(p):
        turn = lax.rem(p, 2)
        block = beside + (above - beside) * turn
        return block_copy(3, p, block, above + (beside - above) * turn)

    def forward(p):
        if square:
            block_copy(1 + lax.rem(p, 2), p, g, beside).wait_recv()
            forward_copy(p).start()

    def arrived(p):
        if square:
            block_copy(2 - lax.rem(p, 2), p, g, beside).wait_recv()
            block_copy(3, p, g, beside).wait_recv()
        else:
            for copy in own_copies(p):
                copy.wait_recv()

    def second_step(p, carry):
        res = advance(mid[:, p], mid[:, p + 1], mid[:, p + 2], *coefficients(p + 1))
        every[g, units(p)] = jnp.swapaxes(res, 0, 1)
        ret[:, p] = res
        return carry

    def inner_step(p, carry):
        second_step(p, carry)
        for copy in own_copies(p):
            copy.start()
        return carry

    for copy in loads[4:]:
        copy.wait()
    lax.fori_loop(2, planes, first_step, 0)
    pl.semaphore_wait(barrier, slabs + groups - 2)

    def halo(sign, k, src, dst):
        return pltpu.make_async_remote_copy(
            src_ref=src,
            dst_ref=dst,
            send_sem=halo_send.at[(sign + 1) // 2, k],
            recv_sem=halo_recv.at[(sign + 1) // 2, k],
            device_id=(g, lax.rem(s + sign + slabs, slabs)),
            device_id_type=MESH,
        )

    up = [
        halo(1, 0, fields_ref.at[:, planes - 2 : planes], ext.at[:, 0:2]),
        halo(1, 1, vel_ref.at[:, planes - 1 : planes], velx.at[:, 0:1]),
        halo(1, 2, dif_ref.at[planes - 1 : planes], difx.at[0:1]),
    ]
    down = [
        halo(-1, 0, fields_ref.at[:, 0:2], ext.at[:, last : last + 2]),
        halo(-1, 1, vel_ref.at[:, 0:1], velx.at[:, planes + 1 : planes + 2]),
        halo(-1, 2, dif_ref.at[0:1], difx.at[planes + 1 : planes + 2]),
    ]

    @pl.when(s < slabs - 1)
    def _():
        for copy in up:
            copy.start()

    @pl.when(s > 0)
    def _():
        for copy in down:
            copy.start()

    lax.fori_loop(2, planes - 2, inner_step, 0)

    for copy in loads[0:4]:
        copy.wait()
    slots = off_ref.shape[1]
    low = off_ref[...] % bt.shape[0]
    high_row = off_ref[...] // bt.shape[0]
    spread_low(bt, jnp.broadcast_to(low.astype(jnp.float32), (TILE, slots)).astype(jnp.bfloat16))

    noise = noise_ref[...]
    slot = lax.broadcasted_iota(jnp.int32, noise.shape, 1)
    inverse = jnp.where(slot < count_ref[0], 1.0 / noise, 0.0)
    first, second = split_two((obs_ref[...] / noise + pert_ref[...]) * inverse)
    both[0:members, :] = first.astype(jnp.bfloat16)
    both[members : 2 * members, :] = second.astype(jnp.bfloat16)
    high[...] = jnp.broadcast_to(high_row.astype(jnp.float32), (TILE, slots)).astype(jnp.bfloat16)
    scatter_weights(high_row, inverse * inverse, bt, w_ref)
    @pl.when(s == 0)
    def _():
        ext[:, 0:2] = jnp.zeros((members, 2, ys, xsz), jnp.float32)
        velx[:, 0:1] = jnp.zeros((3, 1, ys, xsz), jnp.int32)
        difx[0:1] = jnp.zeros((1, ys, xsz), jnp.float32)

    @pl.when(s == slabs - 1)
    def _():
        ext[:, last : last + 2] = jnp.zeros((members, 2, ys, xsz), jnp.float32)
        velx[:, planes + 1 : planes + 2] = jnp.zeros((3, 1, ys, xsz), jnp.int32)
        difx[planes + 1 : planes + 2] = jnp.zeros((1, ys, xsz), jnp.float32)

    @pl.when(s > 0)
    def _():
        for copy in up:
            copy.wait_recv()

    @pl.when(s < slabs - 1)
    def _():
        for copy in down:
            copy.wait_recv()

    lax.fori_loop(0, 2, first_step, 0)
    lax.fori_loop(planes, planes + 2, first_step, 0)

    @pl.when(s == 0)
    def _():
        mid[:, 0] = jnp.zeros((members, ys, xsz), jnp.float32)

    @pl.when(s == slabs - 1)
    def _():
        mid[:, planes + 1] = jnp.zeros((members, ys, xsz), jnp.float32)

    lax.fori_loop(planes - 2, planes, second_step, 0)
    lax.fori_loop(0, 2, second_step, 0)
    edges = [planes - 2, planes - 1, 0, 1]
    if square:
        for p, q in zip(edges[0::2] + edges[1::2], edges[1::2] + edges[0::2]):
            block_copy(1, p, g, beside).start()
            block_copy(2, q, g, above).start()
    else:
        for p in edges:
            for copy in own_copies(p):
                copy.start()

    per = planes * ys // PIECES

    def scatter_turn(q):

        def store(u, value):
            v_ref[q * per + u] = value

        scatter_group(jnp.int32(q), high, both, bt, a2, store)

    forward(2)
    for q in range(PIECES):
        if q < planes - 5:
            forward(q + 3)
        scatter_turn(q)
    for p in edges:
        forward(p)

    ratio = w_ref.shape[0]
    total_rows = order + members
    acc[...] = jnp.zeros(acc.shape, jnp.float32)

    def plane_sums(i, carry):
        p = lax.rem(i + 2, planes)
        arrived(p)
        base = p * ys * xsz
        for u in range(ys):
            unit = p * ys + u
            x = every[:, unit].reshape(order, xsz)
            mean = jnp.sum(x, axis=0, keepdims=True) / order
            w = w_ref[u % ratio, pl.ds(p * (ys // ratio) + u // ratio, 1), :]
            means[pl.ds(unit, 1), :] = mean
            mine = every[g, unit]
            centered = x - mean
            first, second = split_two(centered)
            upper, lower = split_two(
                jnp.concatenate([centered * w, v_ref[unit] - mine * w], axis=0)
            )
            lanes = pl.ds(pl.multiple_of(base + u * xsz, xsz), xsz)
            xs[0:order, lanes] = first.astype(jnp.bfloat16)
            xs[order : 2 * order, lanes] = second.astype(jnp.bfloat16)
            rhs[0:total_rows, u * xsz : (u + 1) * xsz] = upper.astype(jnp.bfloat16)
            rhs[total_rows:, u * xsz : (u + 1) * xsz] = lower.astype(jnp.bfloat16)
        acc[...] += lax.dot_general(
            rhs[...],
            xs[:, pl.ds(pl.multiple_of(base, ys * xsz), ys * xsz)],
            NT,
            preferred_element_type=jnp.float32,
        )
        return carry

    lax.fori_loop(0, planes, plane_sums, 0)

    mine = (acc[0:total_rows] + acc[total_rows:]) / (order - 1)
    mine = mine[:, 0:order] + mine[:, order:]
    pieces = [mine[0:order], mine[order:]]
    folds = 2 if order < LANES else 1
    if folds == 2:
        pieces = [
            jnp.concatenate([a[: a.shape[0] // 2], a[a.shape[0] // 2 :]], axis=1) for a in pieces
        ]
    core, z = lax.rem(s, 2), lax.div(s, 2)
    heights = slabs // 2
    pair[core] = jnp.concatenate(pieces, axis=0)

    def sum_copy(ref, place, sem, r, peer):
        return pltpu.make_async_remote_copy(
            src_ref=ref.at[place],
            dst_ref=ref.at[place],
            send_sem=sem[0].at[r],
            recv_sem=sem[1].at[r],
            device_id=(g, peer),
            device_id_type=MESH,
        )

    pair_copy = sum_copy(pair, core, (ss_sem, sr_sem), 0, s + 1 - 2 * core)
    pair_copy.start()
    pair_copy.wait_recv()
    sums[z] = pair[0] + pair[1]
    s_copies = [
        sum_copy(sums, z, (ss_sem, sr_sem), r, lax.rem(z + r, heights) * 2 + core)
        for r in range(1, heights)
    ]
    for copy in s_copies:
        copy.start()

    def sent_plane(p, carry):
        for copy in own_copies(p):
            copy.wait_send()
        if square:
            forward_copy(p).wait_send()
        return carry

    lax.fori_loop(0, planes, sent_plane, 0)
    pair_copy.wait_send()

    @pl.when(s < slabs - 1)
    def _():
        for copy in up:
            copy.wait_send()

    @pl.when(s > 0)
    def _():
        for copy in down:
            copy.wait_send()

    for copy in s_copies:
        copy.wait()
    added = sums[0]
    for i in range(1, heights):
        added = added + sums[i]

    width = m_ref.shape[1]
    gram, cross = added[0 : order // folds], added[order // folds :]
    if folds == 2:
        gram, cross = [
            jnp.concatenate([a[:, 0:order], a[:, order:]], axis=0) for a in (gram, cross)
        ]
    diagonal = lax.broadcasted_iota(jnp.int32, gram.shape, 0) == lax.broadcasted_iota(
        jnp.int32, gram.shape, 1
    )
    spare = jnp.zeros((width - order - members, order), jnp.float32)
    cross = jnp.concatenate([cross, spare], axis=0).T
    m_ref[...] = jnp.concatenate([gram + jnp.where(diagonal, 1.0, 0.0), cross], axis=1)
    solve_in_place(m_ref)

    weights = m_ref[...].T[0:members]
    total[...] = jnp.broadcast_to(jnp.sum(weights, axis=1, keepdims=True), total.shape)
    left[...] = jnp.concatenate(
        [jnp.concatenate([half, half], axis=1) for half in split_two(weights)], axis=0
    ).astype(jnp.bfloat16)


def finish_kernel(ret, xs, means, left, total, out_hbm, stage, sem):
    members, planes, ys, xsz = out_hbm.shape
    copies = []
    for p in range(planes):
        lanes = slice(p * ys * xsz, (p + 1) * ys * xsz)
        res = lax.dot_general(
            left[...], xs[:, lanes], NN, preferred_element_type=jnp.float32
        )
        res = res[0:members] + res[members:]
        new = [
            res[:, u * xsz : (u + 1) * xsz] + total[...] * means[p * ys + u : p * ys + u + 1, :]
            for u in range(ys)
        ]
        stage[:, p] = ret[:, p] + jnp.swapaxes(jnp.stack(new, axis=0), 0, 1)
        copies.append(pltpu.make_async_copy(stage.at[:, p], out_hbm.at[:, p], sem.at[p]))
        copies[-1].start()
    for copy in copies:
        copy.wait()


def local(
    groups,
    slabs,
    fields,
    velocity,
    diffusivity,
    sensor_offsets,
    sensor_counts,
    observations,
    noise_scale,
    perturbation,
):
    members, planes, ys, xsz = fields.shape
    units = planes * ys
    order = members * groups
    slots = sensor_offsets.shape[0]
    low = 2 * LANES
    highs = units * xsz // low
    width = -(-(order + members) // LANES) * LANES
    folds = 2 if order < LANES else 1
    folded = ((order + members) // folds, order * folds)
    vmem = pl.BlockSpec(memory_space=pltpu.VMEM)
    f32 = jnp.float32
    scratch = [
        pltpu.VMEM((1, slots), jnp.int32),
        pltpu.VMEM((1, slots), f32),
        pltpu.VMEM((1, slots), f32),
        pltpu.VMEM((members, slots), f32),
        pltpu.VMEM((low, slots), jnp.bfloat16),
        pltpu.VMEM((highs // PIECES * 2 * members, slots), jnp.bfloat16),
        pltpu.VMEM((2 * members, slots), jnp.bfloat16),
        pltpu.VMEM((TILE, slots), jnp.bfloat16),
        pltpu.VMEM((units, members, xsz), f32),
        pltpu.VMEM((low // LANES, highs, LANES), f32),
        pltpu.VMEM((members, planes + 4, ys, xsz), f32),
        pltpu.VMEM((3, planes + 2, ys, xsz), jnp.int32),
        pltpu.VMEM((planes + 2, ys, xsz), f32),
        pltpu.VMEM((members, planes + 2, ys, xsz), f32),
        pltpu.VMEM((groups, units, members, xsz), f32),
        pltpu.VMEM((2 * (order + members), ys * xsz), jnp.bfloat16),
        pltpu.VMEM((2 * (order + members), 2 * order), f32),
        pltpu.VMEM((2,) + folded, f32),
        pltpu.VMEM((slabs // 2,) + folded, f32),
        pltpu.VMEM((order, width), f32),
        pltpu.SemaphoreType.DMA((7,)),
        pltpu.SemaphoreType.DMA((2, 3)),
        pltpu.SemaphoreType.DMA((2, 3)),
        pltpu.SemaphoreType.DMA((groups, planes)),
        pltpu.SemaphoreType.DMA((groups, planes)),
        pltpu.SemaphoreType.DMA((slabs // 2,)),
        pltpu.SemaphoreType.DMA((slabs // 2,)),
    ]
    hbm = pl.BlockSpec(memory_space=pltpu.HBM)
    results = [
        pltpu.VMEM(fields.shape, f32),
        pltpu.VMEM((2 * order, units * xsz), jnp.bfloat16),
        pltpu.VMEM((units, xsz), f32),
        pltpu.VMEM((2 * members, 2 * order), jnp.bfloat16),
        pltpu.VMEM((members, xsz), f32),
    ]
    held = sum(math.prod(r.shape) * jnp.dtype(r.dtype).itemsize for r in results)
    room = 58 * 1024 * 1024 - held
    results = pl.pallas_call(
        functools.partial(step_kernel, groups, slabs),
        out_shape=results,
        in_specs=[pl.BlockSpec(memory_space=pltpu.SMEM)] + [hbm] * 7,
        out_specs=[vmem] * len(results),
        scratch_shapes=scratch,
        compiler_params=pltpu.CompilerParams(
            collective_id=0, has_side_effects=True, vmem_limit_bytes=room
        ),
        name="ensemble_step",
    )(
        sensor_counts,
        sensor_offsets[None],
        observations[None],
        noise_scale[None],
        perturbation,
        fields,
        velocity,
        diffusivity,
    )
    return pl.pallas_call(
        finish_kernel,
        out_shape=jax.ShapeDtypeStruct(fields.shape, f32),
        in_specs=[vmem] * len(results),
        out_specs=hbm,
        scratch_shapes=[
            pltpu.VMEM(fields.shape, f32),
            pltpu.SemaphoreType.DMA((planes,)),
        ],
        compiler_params=pltpu.CompilerParams(vmem_limit_bytes=16 * 1024 * 1024),
        name="finish",
    )(*results)


def solution(mesh):
    return jax.shard_map(
        functools.partial(local, mesh.shape["grp"], mesh.shape["slab"]),
        mesh=mesh,
        in_specs=(
            P("grp", "slab", None, None),
            P(None, "slab", None, None),
            P("slab", None, None),
            P("slab"),
            P("slab"),
            P("slab"),
            P("slab"),
            P("grp", "slab"),
        ),
        out_specs=P("grp", "slab", None, None),
        check_vma=False,
    )
```

```python
import functools
import math

import jax
import jax.numpy as jnp
from jax import lax
from jax.experimental import pallas as pl
from jax.experimental.pallas import tpu as pltpu
from jax.sharding import PartitionSpec as P

STEPS = 2
COURANT = 0.12
PIECES = 4
TILE = 16
LANES = 128
BLOCK = 8
MESH = pl.DeviceIdType.MESH
NT = (((1,), (1,)), ((), ()))
NN = (((1,), (0,)), ((), ()))


def split_two(values):
    high = values.astype(jnp.bfloat16).astype(jnp.float32)
    return high, values - high


def spread_low(bt, low):
    rows = lax.broadcasted_iota(jnp.int32, low.shape, 0).astype(jnp.float32)
    one, zero = jnp.bfloat16(1.0), jnp.bfloat16(0.0)
    for r in range(0, bt.shape[0], TILE):
        wanted = (rows + r).astype(jnp.bfloat16)
        bt[r : r + TILE, :] = jnp.where(low == wanted, one, zero)


def scatter_group(q, high, both, bt, a2, store):
    rows = both.shape[0]
    members = rows // 2
    per_group = a2.shape[0] // rows
    ratio = bt.shape[0] // LANES
    zero = jnp.bfloat16(0.0)
    for k in range(per_group):
        wanted = (q * per_group + k).astype(jnp.float32).astype(jnp.bfloat16)
        for t in range(0, rows, TILE):
            a2[k * rows + t : k * rows + t + TILE, :] = jnp.where(
                high[...] == wanted, both[t : t + TILE, :], zero
            )
    res = lax.dot_general(a2[...], bt[...], NT, preferred_element_type=jnp.float32)
    for k in range(per_group):
        start = k * rows
        added = res[start : start + members] + res[start + members : start + rows]
        for i in range(ratio):
            store(k * ratio + i, added[:, i * LANES : (i + 1) * LANES])


def scatter_weights(high, weight, bt, w_ref):
    rows = w_ref.shape[1]
    wanted = lax.broadcasted_iota(jnp.int32, (rows, high.shape[1]), 0)
    first, second = split_two(jnp.where(wanted == high, weight, 0.0))
    stacked = jnp.concatenate([first, second], axis=0).astype(jnp.bfloat16)
    res = lax.dot_general(stacked, bt[...], NT, preferred_element_type=jnp.float32)
    total = res[:rows] + res[rows:]
    for i in range(w_ref.shape[0]):
        w_ref[i] = total[:, i * LANES : (i + 1) * LANES]


def upwind(courant, center, lower_side, upper_side):
    return jnp.maximum(courant, 0.0) * (center - lower_side) + jnp.minimum(courant, 0.0) * (
        upper_side - center
    )


def advance(below, center, above, cz, cy, cx, diffusivity):
    y_size, x_size = center.shape[1:]
    south = pltpu.roll(center, 1, 1)
    north = pltpu.roll(center, y_size - 1, 1)
    west = pltpu.roll(center, 1, 2)
    east = pltpu.roll(center, x_size - 1, 2)
    transport = upwind(cz, center, below, above) + upwind(cy, center, south, north)
    transport = transport + upwind(cx, center, west, east)
    laplace = below + above + south + north + west + east - 6.0 * center
    return center - transport + diffusivity * laplace


def solve_transposed(m_ref, columns):
    order, width = m_ref.shape

    def reduced(whole, rows, at):
        row_id = lax.broadcasted_iota(jnp.int32, rows.shape, 0)
        cols = [jnp.broadcast_to(rows[:, at + i : at + i + 1], rows.shape) for i in range(BLOCK)]
        for j in range(0, BLOCK, 2):
            k = j + 1
            left, right = cols[j], cols[k]
            a, b, c, d = left[j:k, :], right[j:k, :], left[k : k + 1, :], right[k : k + 1, :]
            inverse = 1.0 / (a * d - b * c)

            def eliminate(t):
                upper, lower = t[j:k, :], t[k : k + 1, :]
                first = (d * upper - b * lower) * inverse
                second = (a * lower - c * upper) * inverse
                rest = t - left * first - right * second
                return jnp.where(row_id == j, first, jnp.where(row_id == k, second, rest))

            rows = eliminate(rows)
            for i in range(j + 2, BLOCK):
                cols[i] = eliminate(cols[i])
        new = whole
        for j in range(BLOCK):
            new = new - whole[:, at + j : at + j + 1] * rows[j : j + 1, :]
        return new, rows

    if order < LANES:
        whole = m_ref[...]
        for start in range(0, order, BLOCK):
            stop = start + BLOCK
            new, rows = reduced(whole, whole[start:stop], start)
            kept = [new[:start]] if start else []
            kept += [rows] + ([new[stop:]] if stop < order else [])
            whole = jnp.concatenate(kept, axis=0)
        return whole.T[order : order + columns]

    def block(b, carry):
        start = pl.multiple_of(b * BLOCK, BLOCK)
        new, rows = reduced(m_ref[...], m_ref[pl.ds(start, BLOCK), :], 0)
        m_ref[...] = pltpu.roll(new, width - BLOCK, 1)
        m_ref[pl.ds(start, BLOCK), :] = pltpu.roll(rows, width - BLOCK, 1)
        return carry

    lax.fori_loop(0, order // BLOCK, block, 0)
    return m_ref[...].T[0:columns]


def step_kernel(
    groups,
    slabs,
    count_ref,
    off_hbm,
    obs_hbm,
    noise_hbm,
    pert_hbm,
    fields_ref,
    vel_ref,
    dif_ref,
    ret,
    xs,
    means,
    left,
    total,
    off_ref,
    obs_ref,
    noise_ref,
    pert_ref,
    bt,
    a2,
    both,
    high,
    v_ref,
    w_ref,
    ext,
    velx,
    difx,
    mid,
    every,
    rhs,
    acc,
    pair,
    sums,
    m_ref,
    local_sem,
    halo_send,
    halo_recv,
    es_sem,
    er_sem,
    ss_sem,
    sr_sem,
):
    g, s = lax.axis_index("grp"), lax.axis_index("slab")
    members, planes, ys, xsz = fields_ref.shape
    order = members * groups
    last = planes + STEPS

    loads = [
        pltpu.make_async_copy(source, target, local_sem.at[i])
        for i, (source, target) in enumerate(
            (
                (off_hbm, off_ref),
                (noise_hbm, noise_ref),
                (obs_hbm, obs_ref),
                (pert_hbm, pert_ref),
                (fields_ref, ext.at[:, 2:last]),
                (vel_ref, velx.at[:, 1 : planes + 1]),
                (dif_ref, difx.at[1 : planes + 1]),
            )
        )
    ]
    for copy in loads[4:] + loads[:4]:
        copy.start()

    def group_peer(r):
        return (lax.rem(g + r, groups), s)

    def slab_peer(r):
        return (g, lax.rem(s + r, slabs))

    barrier = pltpu.get_barrier_semaphore()
    for r in range(1, slabs):
        pl.semaphore_signal(barrier, inc=1, device_id=slab_peer(r), device_id_type=MESH)
    for r in range(1, groups):
        pl.semaphore_signal(barrier, inc=1, device_id=group_peer(r), device_id_type=MESH)

    def coefficients(p):
        courant = [velx[c, p].astype(jnp.float32)[None] * COURANT for c in range(3)]
        return courant + [difx[p][None]]

    def first_step(p, carry):
        mid[:, p] = advance(ext[:, p], ext[:, p + 1], ext[:, p + 2], *coefficients(p))
        return carry

    def units(p):
        return pl.ds(p * ys, ys)

    square = groups == 4
    beside = g + 1 - 2 * lax.rem(g, 2)
    above = lax.rem(g + 2, groups)

    def block_copy(kind, p, block, peer):
        return pltpu.make_async_remote_copy(
            src_ref=every.at[block, units(p)],
            dst_ref=every.at[block, units(p)],
            send_sem=es_sem.at[kind, p],
            recv_sem=er_sem.at[kind, p],
            device_id=(peer, s),
            device_id_type=MESH,
        )

    def own_copies(p):
        if square:
            return [block_copy(1, p, g, beside), block_copy(2, p, g, above)]
        return [block_copy(r, p, g, lax.rem(g + r, groups)) for r in range(1, groups)]

    def forward_copy(p):
        turn = lax.rem(p, 2)
        block = beside + (above - beside) * turn
        return block_copy(3, p, block, above + (beside - above) * turn)

    def forward(p):
        if square:
            block_copy(1 + lax.rem(p, 2), p, g, beside).wait_recv()
            forward_copy(p).start()

    def arrived(p):
        if square:
            block_copy(2 - lax.rem(p, 2), p, g, beside).wait_recv()
            block_copy(3, p, g, beside).wait_recv()
        else:
            for copy in own_copies(p):
                copy.wait_recv()

    def second_step(p, carry):
        res = advance(mid[:, p], mid[:, p + 1], mid[:, p + 2], *coefficients(p + 1))
        every[g, units(p)] = jnp.swapaxes(res, 0, 1)
        ret[:, p] = res
        return carry

    def inner_step(p, carry):
        second_step(p, carry)
        for copy in own_copies(p):
            copy.start()
        return carry

    for copy in loads[4:]:
        copy.wait()
    lax.fori_loop(2, planes, first_step, 0)
    pl.semaphore_wait(barrier, slabs + groups - 2)

    def halo(sign, k, src, dst):
        return pltpu.make_async_remote_copy(
            src_ref=src,
            dst_ref=dst,
            send_sem=halo_send.at[(sign + 1) // 2, k],
            recv_sem=halo_recv.at[(sign + 1) // 2, k],
            device_id=(g, lax.rem(s + sign + slabs, slabs)),
            device_id_type=MESH,
        )

    up = [
        halo(1, 0, fields_ref.at[:, planes - 2 : planes], ext.at[:, 0:2]),
        halo(1, 1, vel_ref.at[:, planes - 1 : planes], velx.at[:, 0:1]),
        halo(1, 2, dif_ref.at[planes - 1 : planes], difx.at[0:1]),
    ]
    down = [
        halo(-1, 0, fields_ref.at[:, 0:2], ext.at[:, last : last + 2]),
        halo(-1, 1, vel_ref.at[:, 0:1], velx.at[:, planes + 1 : planes + 2]),
        halo(-1, 2, dif_ref.at[0:1], difx.at[planes + 1 : planes + 2]),
    ]

    @pl.when(s < slabs - 1)
    def _():
        for copy in up:
            copy.start()

    @pl.when(s > 0)
    def _():
        for copy in down:
            copy.start()

    lax.fori_loop(2, planes - 2, inner_step, 0)

    for copy in loads[0:4]:
        copy.wait()
    slots = off_ref.shape[1]
    low = off_ref[...] % bt.shape[0]
    high_row = off_ref[...] // bt.shape[0]
    spread_low(bt, jnp.broadcast_to(low.astype(jnp.float32), (TILE, slots)).astype(jnp.bfloat16))

    noise = noise_ref[...]
    slot = lax.broadcasted_iota(jnp.int32, noise.shape, 1)
    inverse = jnp.where(slot < count_ref[0], 1.0 / noise, 0.0)
    first, second = split_two((obs_ref[...] / noise + pert_ref[...]) * inverse)
    both[0:members, :] = first.astype(jnp.bfloat16)
    both[members : 2 * members, :] = second.astype(jnp.bfloat16)
    high[...] = jnp.broadcast_to(high_row.astype(jnp.float32), (TILE, slots)).astype(jnp.bfloat16)
    scatter_weights(high_row, inverse * inverse, bt, w_ref)
    @pl.when(s == 0)
    def _():
        ext[:, 0:2] = jnp.zeros((members, 2, ys, xsz), jnp.float32)
        velx[:, 0:1] = jnp.zeros((3, 1, ys, xsz), jnp.int32)
        difx[0:1] = jnp.zeros((1, ys, xsz), jnp.float32)

    @pl.when(s == slabs - 1)
    def _():
        ext[:, last : last + 2] = jnp.zeros((members, 2, ys, xsz), jnp.float32)
        velx[:, planes + 1 : planes + 2] = jnp.zeros((3, 1, ys, xsz), jnp.int32)
        difx[planes + 1 : planes + 2] = jnp.zeros((1, ys, xsz), jnp.float32)

    @pl.when(s > 0)
    def _():
        for copy in up:
            copy.wait_recv()

    @pl.when(s < slabs - 1)
    def _():
        for copy in down:
            copy.wait_recv()

    lax.fori_loop(0, 2, first_step, 0)
    lax.fori_loop(planes, planes + 2, first_step, 0)

    @pl.when(s == 0)
    def _():
        mid[:, 0] = jnp.zeros((members, ys, xsz), jnp.float32)

    @pl.when(s == slabs - 1)
    def _():
        mid[:, planes + 1] = jnp.zeros((members, ys, xsz), jnp.float32)

    lax.fori_loop(planes - 2, planes, second_step, 0)
    lax.fori_loop(0, 2, second_step, 0)
    edges = [planes - 2, planes - 1, 0, 1]
    if square:
        for p, q in zip(edges[0::2] + edges[1::2], edges[1::2] + edges[0::2]):
            block_copy(1, p, g, beside).start()
            block_copy(2, q, g, above).start()
    else:
        for p in edges:
            for copy in own_copies(p):
                copy.start()

    per = planes * ys // PIECES

    def scatter_turn(q):

        def store(u, value):
            v_ref[q * per + u] = value

        scatter_group(jnp.int32(q), high, both, bt, a2, store)

    forward(2)
    for q in range(PIECES):
        if q < planes - 5:
            forward(q + 3)
        scatter_turn(q)
    for p in edges:
        forward(p)

    ratio = w_ref.shape[0]
    total_rows = order + members
    acc[...] = jnp.zeros(acc.shape, jnp.float32)

    def plane_sums(i, carry):
        p = lax.rem(i + 2, planes)
        arrived(p)
        base = p * ys * xsz
        for u in range(ys):
            unit = p * ys + u
            x = every[:, unit].reshape(order, xsz)
            mean = jnp.sum(x, axis=0, keepdims=True) / order
            w = w_ref[u % ratio, pl.ds(p * (ys // ratio) + u // ratio, 1), :]
            means[pl.ds(unit, 1), :] = mean
            mine = every[g, unit]
            centered = x - mean
            first, second = split_two(centered)
            upper, lower = split_two(
                jnp.concatenate([centered * w, v_ref[unit] - mine * w], axis=0)
            )
            lanes = pl.ds(pl.multiple_of(base + u * xsz, xsz), xsz)
            xs[0:order, lanes] = first.astype(jnp.bfloat16)
            xs[order : 2 * order, lanes] = second.astype(jnp.bfloat16)
            rhs[0:total_rows, u * xsz : (u + 1) * xsz] = upper.astype(jnp.bfloat16)
            rhs[total_rows:, u * xsz : (u + 1) * xsz] = lower.astype(jnp.bfloat16)
        acc[...] += lax.dot_general(
            rhs[...],
            xs[:, pl.ds(pl.multiple_of(base, ys * xsz), ys * xsz)],
            NT,
            preferred_element_type=jnp.float32,
        )
        return carry

    lax.fori_loop(0, planes, plane_sums, 0)

    mine = (acc[0:total_rows] + acc[total_rows:]) / (order - 1)
    mine = mine[:, 0:order] + mine[:, order:]
    folded = order < LANES
    half = order // 2
    if folded:
        cross = mine[order:]
        cross = jnp.concatenate([cross[:, 0:half], cross[:, half:]], axis=0)
        mine = jnp.concatenate([mine[0:half], mine[half:order, half:], cross], axis=1)
    core, z = lax.rem(s, 2), lax.div(s, 2)
    heights = slabs // 2
    pair[core] = mine

    def sum_copy(ref, place, sem, r, peer):
        return pltpu.make_async_remote_copy(
            src_ref=ref.at[place],
            dst_ref=ref.at[place],
            send_sem=sem[0].at[r],
            recv_sem=sem[1].at[r],
            device_id=(g, peer),
            device_id_type=MESH,
        )

    pair_copy = sum_copy(pair, core, (ss_sem, sr_sem), 0, s + 1 - 2 * core)
    pair_copy.start()
    pair_copy.wait_recv()
    sums[z] = pair[0] + pair[1]
    s_copies = [
        sum_copy(sums, z, (ss_sem, sr_sem), r, lax.rem(z + r, heights) * 2 + core)
        for r in range(1, heights)
    ]
    for copy in s_copies:
        copy.start()

    def sent_plane(p, carry):
        for copy in own_copies(p):
            copy.wait_send()
        if square:
            forward_copy(p).wait_send()
        return carry

    lax.fori_loop(0, planes, sent_plane, 0)
    pair_copy.wait_send()

    @pl.when(s < slabs - 1)
    def _():
        for copy in up:
            copy.wait_send()

    @pl.when(s > 0)
    def _():
        for copy in down:
            copy.wait_send()

    for copy in s_copies:
        copy.wait()
    added = sums[0]
    for i in range(1, heights):
        added = added + sums[i]

    width = m_ref.shape[1]
    if folded:
        corner = added[:, half:order].T
        gram = jnp.concatenate(
            [
                added[:, 0:order],
                jnp.concatenate([corner, added[:, order : order + half]], axis=1),
            ],
            axis=0,
        )
        cross = added[:, order + half :]
        cross = jnp.concatenate([cross[0:members], cross[members:]], axis=1)
    else:
        gram, cross = added[0:order], added[order:]
    diagonal = lax.broadcasted_iota(jnp.int32, gram.shape, 0) == lax.broadcasted_iota(
        jnp.int32, gram.shape, 1
    )
    spare = jnp.zeros((width - order - members, order), jnp.float32)
    cross = jnp.concatenate([cross, spare], axis=0).T
    m_ref[...] = jnp.concatenate([gram + jnp.where(diagonal, 1.0, 0.0), cross], axis=1)
    weights = solve_transposed(m_ref, members)

    total[...] = jnp.broadcast_to(jnp.sum(weights, axis=1, keepdims=True), total.shape)
    left[...] = jnp.concatenate(
        [jnp.concatenate([half, half], axis=1) for half in split_two(weights)], axis=0
    ).astype(jnp.bfloat16)


def finish_kernel(ret, xs, means, left, total, out_hbm, stage, sem):
    members, planes, ys, xsz = out_hbm.shape
    copies = []
    for p in range(planes):
        lanes = slice(p * ys * xsz, (p + 1) * ys * xsz)
        res = lax.dot_general(
            left[...], xs[:, lanes], NN, preferred_element_type=jnp.float32
        )
        res = res[0:members] + res[members:]
        new = [
            res[:, u * xsz : (u + 1) * xsz] + total[...] * means[p * ys + u : p * ys + u + 1, :]
            for u in range(ys)
        ]
        stage[:, p] = ret[:, p] + jnp.swapaxes(jnp.stack(new, axis=0), 0, 1)
        copies.append(pltpu.make_async_copy(stage.at[:, p], out_hbm.at[:, p], sem.at[p]))
        copies[-1].start()
    for copy in copies:
        copy.wait()


def local(
    groups,
    slabs,
    fields,
    velocity,
    diffusivity,
    sensor_offsets,
    sensor_counts,
    observations,
    noise_scale,
    perturbation,
):
    members, planes, ys, xsz = fields.shape
    units = planes * ys
    order = members * groups
    slots = sensor_offsets.shape[0]
    low = 2 * LANES
    highs = units * xsz // low
    width = -(-(order + members) // LANES) * LANES
    folded = (order // 2, 2 * order) if order < LANES else (order + members, order)
    vmem = pl.BlockSpec(memory_space=pltpu.VMEM)
    f32 = jnp.float32
    scratch = [
        pltpu.VMEM((1, slots), jnp.int32),
        pltpu.VMEM((1, slots), f32),
        pltpu.VMEM((1, slots), f32),
        pltpu.VMEM((members, slots), f32),
        pltpu.VMEM((low, slots), jnp.bfloat16),
        pltpu.VMEM((highs // PIECES * 2 * members, slots), jnp.bfloat16),
        pltpu.VMEM((2 * members, slots), jnp.bfloat16),
        pltpu.VMEM((TILE, slots), jnp.bfloat16),
        pltpu.VMEM((units, members, xsz), f32),
        pltpu.VMEM((low // LANES, highs, LANES), f32),
        pltpu.VMEM((members, planes + 4, ys, xsz), f32),
        pltpu.VMEM((3, planes + 2, ys, xsz), jnp.int32),
        pltpu.VMEM((planes + 2, ys, xsz), f32),
        pltpu.VMEM((members, planes + 2, ys, xsz), f32),
        pltpu.VMEM((groups, units, members, xsz), f32),
        pltpu.VMEM((2 * (order + members), ys * xsz), jnp.bfloat16),
        pltpu.VMEM((2 * (order + members), 2 * order), f32),
        pltpu.VMEM((2,) + folded, f32),
        pltpu.VMEM((slabs // 2,) + folded, f32),
        pltpu.VMEM((order, width), f32),
        pltpu.SemaphoreType.DMA((7,)),
        pltpu.SemaphoreType.DMA((2, 3)),
        pltpu.SemaphoreType.DMA((2, 3)),
        pltpu.SemaphoreType.DMA((groups, planes)),
        pltpu.SemaphoreType.DMA((groups, planes)),
        pltpu.SemaphoreType.DMA((slabs // 2,)),
        pltpu.SemaphoreType.DMA((slabs // 2,)),
    ]
    hbm = pl.BlockSpec(memory_space=pltpu.HBM)
    results = [
        pltpu.VMEM(fields.shape, f32),
        pltpu.VMEM((2 * order, units * xsz), jnp.bfloat16),
        pltpu.VMEM((units, xsz), f32),
        pltpu.VMEM((2 * members, 2 * order), jnp.bfloat16),
        pltpu.VMEM((members, xsz), f32),
    ]
    held = sum(math.prod(r.shape) * jnp.dtype(r.dtype).itemsize for r in results)
    room = 58 * 1024 * 1024 - held
    results = pl.pallas_call(
        functools.partial(step_kernel, groups, slabs),
        out_shape=results,
        in_specs=[pl.BlockSpec(memory_space=pltpu.SMEM)] + [hbm] * 7,
        out_specs=[vmem] * len(results),
        scratch_shapes=scratch,
        compiler_params=pltpu.CompilerParams(
            collective_id=0, has_side_effects=True, vmem_limit_bytes=room
        ),
        name="ensemble_step",
    )(
        sensor_counts,
        sensor_offsets[None],
        observations[None],
        noise_scale[None],
        perturbation,
        fields,
        velocity,
        diffusivity,
    )
    return pl.pallas_call(
        finish_kernel,
        out_shape=jax.ShapeDtypeStruct(fields.shape, f32),
        in_specs=[vmem] * len(results),
        out_specs=hbm,
        scratch_shapes=[
            pltpu.VMEM(fields.shape, f32),
            pltpu.SemaphoreType.DMA((planes,)),
        ],
        compiler_params=pltpu.CompilerParams(vmem_limit_bytes=16 * 1024 * 1024),
        name="finish",
    )(*results)


def solution(mesh):
    return jax.shard_map(
        functools.partial(local, mesh.shape["grp"], mesh.shape["slab"]),
        mesh=mesh,
        in_specs=(
            P("grp", "slab", None, None),
            P(None, "slab", None, None),
            P("slab", None, None),
            P("slab"),
            P("slab"),
            P("slab"),
            P("slab"),
            P("grp", "slab"),
        ),
        out_specs=P("grp", "slab", None, None),
        check_vma=False,
    )
```
